128 devices in a mesh: state: 4 (over y_lo, core), domain: 32 (over z, y_hi, x).
Axes of the slice: x: 4, y: 4 (y_hi: 2, y_lo: 2; y = y_hi * 2 + y_lo), z: 4, core: 2. Of those that a mesh axis runs over, the one named last changes fastest.
Arguments:
- orbitals: float32 [2, 4, 224, 25600], P(None, 'state', 'domain'), may hold values from -6 to 6
- occupation: float32 [4], P('state'), may hold values from 8e-07 to 3.2e-06
- potential: float32 [224, 25600], P('domain'), may hold values from 0 to 2
- background: float32 [224, 25600], P('domain'), may hold values from 0.005 to 270, as said below
- layer_start: int32 [33], replicated, may hold values from 0 to 160, as said below
Outputs:
- orbitals_next: float32 [2, 4, 224, 25600], P(None, 'state', 'domain')
- potential_next: float32 [224, 25600], P('domain')
The draws below stay inside these ranges and needn't reach their ends.
Inputs may be any that keep to these rules, and one draw needn't show every extreme that they name: layer_start[d] - 5 d lies in 0..2, is 0 for the first and the last entry and 2 for the last domain's start, so each domain owns 3 to 7 layers and some domain owns exactly 7. `background`: positive.
All inputs are finite; a program needn't handle non-finite values.
Results may differ from the reference program's by a relative error of at most 0.000071.
Values sent between devices are 32-bit elements; how exact they have to be, the bound alone decides.
A program may use at most 128 MiB of HBM per device.

```python
import math
import jax
import jax.numpy as jnp
from jax import lax

SIDE = 160
SLAB = 5
TERMS = 4
LAYERS = 7
ORBITALS = 4
ROWS = 224
PLANE = 25600
N_DOMAIN = 32


ion_spacing = 8


def draw_layer_start(key, part):
    jitter_key, pick_key = jax.random.split(jax.random.fold_in(key, 7))
    jitter = jax.random.randint(jitter_key, (N_DOMAIN + 1,), 0, 3).astype(jnp.int32)
    widest = jax.random.randint(pick_key, (), 0, N_DOMAIN - 1).astype(jnp.int32)
    slot_ids = jnp.arange(N_DOMAIN + 1, dtype=jnp.int32)
    jitter = jnp.where(slot_ids == widest, 0, jitter)
    jitter = jnp.where(slot_ids == widest + 1, 2, jitter)
    jitter = jnp.where(slot_ids == N_DOMAIN - 1, 2, jitter)
    jitter = jnp.where((slot_ids == 0) | (slot_ids == N_DOMAIN), 0, jitter)
    return (SLAB * slot_ids + jitter).astype(jnp.int32)


def draw_background(key, part):
    starts = draw_layer_start(key, part)
    place_key, charge_key, floor_key = jax.random.split(jax.random.fold_in(key, 11), 3)
    length_cells = SLAB * N_DOMAIN
    slot_ids = jnp.arange(N_DOMAIN * LAYERS, dtype=jnp.int32)
    slot_domain = slot_ids // LAYERS
    slot_x = jnp.minimum(starts[slot_domain] + slot_ids - slot_domain * LAYERS, length_cells - 1).astype(jnp.int32)
    side_cells = jnp.arange(SIDE, dtype=jnp.int32)
    x_blocks = (length_cells + ion_spacing - 1) // ion_spacing
    side_blocks = (SIDE + ion_spacing - 1) // ion_spacing
    offsets = jax.random.randint(place_key, (3, x_blocks, side_blocks, side_blocks), 0, ion_spacing).astype(jnp.int32)
    charges = jax.random.uniform(charge_key, (x_blocks, side_blocks, side_blocks), jnp.float32, 0.5, 1.5)
    block_x = (slot_x // ion_spacing)[:, None, None]
    block_y = (side_cells // ion_spacing)[None, :, None]
    block_z = (side_cells // ion_spacing)[None, None, :]
    ion_cell = offsets[0][block_x, block_y, block_z] == (slot_x % ion_spacing)[:, None, None]
    ion_cell = ion_cell & (offsets[1][block_x, block_y, block_z] == (side_cells % ion_spacing)[None, :, None])
    ion_cell = ion_cell & (offsets[2][block_x, block_y, block_z] == (side_cells % ion_spacing)[None, None, :])
    ion_charge = charges[block_x, block_y, block_z]
    rising = slot_x.astype(jnp.float32) / length_cells
    uniform_floor = jax.random.uniform(floor_key, (N_DOMAIN * LAYERS, SIDE, SIDE), jnp.float32, 0.5, 1.5)
    gradient = 1.0 + 2.0 * rising
    floor_part = 0.01 * uniform_floor
    ion_part = jnp.where(ion_cell, 20.0 * ion_charge, 0.0)
    values = (floor_part + ion_part) * gradient[:, None, None]
    return values.reshape(N_DOMAIN * LAYERS, SIDE * SIDE).astype(jnp.float32)


def shard_levels(own_key, dims, cuts, smallest, high):
    def one(axis_at, blocks):
        steps = jax.random.uniform(jax.random.fold_in(jax.random.fold_in(own_key, 6), axis_at), (blocks,), jnp.float32, smallest / len(cuts), high / len(cuts))
        return jnp.repeat(jnp.exp(steps), dims[axis_at] // blocks).reshape((-1,) + (1,) * (len(dims) - axis_at - 1))

    gain = one(*cuts[0])
    for cut in cuts[1:]:
        gain = gain * one(*cut)
    return gain


def normal_values(rng, dims, spread, reach, pieces=(), kind=jnp.bfloat16):
    entries = spread * jax.random.normal(rng, dims, jnp.float32)
    if pieces:
        entries = entries * shard_levels(rng, dims, pieces, -0.22, 0.18)
    return jnp.clip(entries, -reach, reach).astype(kind)


def setup_inputs(seed: int = 0) -> dict:
    key_of = jax.random.split(jax.random.key(seed), 6)
    orbitals = normal_values(key_of[0], (2, ORBITALS, ROWS, PLANE), 1.0, 6.0, ((1, 4), (2, 32)), jnp.float32)
    occupation = jnp.clip(8.000000093488779e-07 + 2.400000028046634e-06 * jax.random.uniform(key_of[1], (ORBITALS,), jnp.float32) ** shard_levels(key_of[1], (ORBITALS,), ((0, 4),), -0.2, 0.2), 8.000000093488779e-07, 3.2000000373955118e-06)
    potential = jnp.clip(2.0 * jax.random.uniform(key_of[2], (ROWS, PLANE), jnp.float32) ** shard_levels(key_of[2], (ROWS, PLANE), ((0, 32),), -0.2, 0.2), 0.0, 2.0)
    background = draw_background(jax.random.fold_in(key_of[5], 71), 0)
    layer_start = draw_layer_start(jax.random.fold_in(key_of[5], 71), 0)
    return {"orbitals": orbitals, "occupation": occupation, "potential": potential, "background": background, "layer_start": layer_start}


time_step = 0.3
four_pi = 4.0 * math.pi
two_pi = 2.0 * math.pi


def inside_mask(x_rows, edge_cells, length_cells):
    along_x = (2 * x_rows - (length_cells - 1)) ** 2 * ((edge_cells - 2) ** 2)
    across = 2 * jnp.arange(edge_cells, dtype=jnp.int32) - (edge_cells - 1)
    circle = (across[:, None] ** 2 + across[None, :] ** 2) * ((length_cells - 2) ** 2)
    return along_x[:, None, None] + circle[None] <= (length_cells - 2) ** 2 * (edge_cells - 2) ** 2


def wave_squared(count_cells):
    index_run = jnp.arange(count_cells, dtype=jnp.int32)
    folded = jnp.where(2 * index_run <= count_cells, index_run, index_run - count_cells)
    wave_number = folded.astype(jnp.float32) * (two_pi / count_cells)
    return wave_number * wave_number


def hamilton(grid_field, local_potential):
    padded = jnp.pad(grid_field, 1)
    beside = padded[:-2, 1:-1, 1:-1] + padded[2:, 1:-1, 1:-1]
    beside = beside + padded[1:-1, :-2, 1:-1] + padded[1:-1, 2:, 1:-1]
    beside = beside + padded[1:-1, 1:-1, :-2] + padded[1:-1, 1:-1, 2:]
    return 0.5 * (6.0 * grid_field - beside) + local_potential * grid_field


def reference(orbitals, occupation, potential, background, layer_start):
    length_cells = SLAB * N_DOMAIN
    x_cells = jnp.arange(length_cells, dtype=jnp.int32)
    owner_domain = jnp.sum((layer_start[None, 1:N_DOMAIN] <= x_cells[:, None]).astype(jnp.int32), axis=1).astype(jnp.int32)
    row_of_x = (owner_domain * LAYERS + x_cells - layer_start[owner_domain]).astype(jnp.int32)
    slot_ids = jnp.arange(N_DOMAIN * LAYERS, dtype=jnp.int32)
    slot_domain = slot_ids // LAYERS
    slot_x = layer_start[slot_domain] + slot_ids - slot_domain * LAYERS
    slot_valid = slot_x < layer_start[slot_domain + 1]
    slot_clip = jnp.minimum(slot_x, length_cells - 1).astype(jnp.int32)
    sphere_mask = inside_mask(x_cells, SIDE, length_cells).astype(jnp.float32)
    cube_potential = jnp.take(potential, row_of_x, axis=0).reshape(length_cells, SIDE, SIDE)

    def to_cube(stored):
        return jnp.take(stored, row_of_x, axis=0).reshape(length_cells, SIDE, SIDE) * sphere_mask

    def to_slots(cube_values):
        flattened = cube_values.reshape(length_cells, SIDE * SIDE)
        return jnp.where(slot_valid[:, None], jnp.take(flattened, slot_clip, axis=0), 0.0)

    def propagate(density, inputs):
        orbital_pair, weight = inputs
        current = jnp.stack([to_cube(orbital_pair[0]), to_cube(orbital_pair[1])])
        summed = current
        for term_order in range(1, TERMS + 1):
            factor = time_step / term_order
            applied_real = hamilton(current[0], cube_potential) * sphere_mask
            applied_imag = hamilton(current[1], cube_potential) * sphere_mask
            current = jnp.stack([factor * applied_imag, -factor * applied_real])
            summed = summed + current
        density = density + weight * (summed[0] * summed[0] + summed[1] * summed[1])
        return density, jnp.stack([to_slots(summed[0]), to_slots(summed[1])])

    empty_density = jnp.zeros((length_cells, SIDE, SIDE), jnp.float32)
    density, propagated = lax.scan(propagate, empty_density, (jnp.swapaxes(orbitals, 0, 1), occupation))
    ion_cube = to_cube(background)
    neutral_scale = jnp.sum(density) / jnp.sum(ion_cube)
    charge = density - neutral_scale * ion_cube
    squared = wave_squared(length_cells)[:, None, None] + wave_squared(SIDE)[None, :, None] + wave_squared(SIDE)[None, None, :]
    kernel_values = jnp.where(squared > 0, four_pi / jnp.where(squared > 0, squared, 1.0), 0.0)
    hartree = jnp.real(jnp.fft.ifftn(jnp.fft.fftn(charge) * kernel_values))
    field_cube = (hartree - jnp.cbrt(3.0 * density / math.pi)) * sphere_mask
    return jnp.swapaxes(propagated, 0, 1), to_slots(field_cube)
```

```python
import functools
import math

import jax
import jax.numpy as jnp
import numpy as np
from jax import lax
from jax.experimental import pallas as pl
from jax.experimental.pallas import tpu as pltpu
from jax.sharding import PartitionSpec as P

SIDE = 160
SLAB = 5
TERMS = 4
LAYERS = 7
PLANE = SIDE * SIDE
GROUPS = 40
LANES = 640
CHUNKS = 5
CHUNK_GROUPS = 8
OWNERS = 100
PAIRS = 50
DOMAINS = 32
STATES = 4
CHIPS = 64

time_step = 0.3
four_pi = 4.0 * math.pi
two_pi = 2.0 * math.pi
MESH = pl.DeviceIdType.MESH
f32 = jnp.float32
i32 = jnp.int32
bf16 = jnp.bfloat16


def halves(table):
    table = np.asarray(table, np.float32)
    high = table.astype(bf16)
    low = (table - high.astype(np.float32)).astype(bf16)
    return np.stack([high, low])


def real_basis():
    n = SIDE
    j = np.arange(n)
    rows = []
    for i in range(n):
        if i == 0:
            rows.append(np.full(n, math.sqrt(1.0 / n)))
        elif i < n // 2:
            rows.append(math.sqrt(2.0 / n) * np.cos(2 * np.pi * ((i * j) % n) / n))
        elif i == n // 2:
            rows.append(math.sqrt(1.0 / n) * np.where(j % 2 == 0, 1.0, -1.0))
        else:
            m = i - n // 2
            rows.append(math.sqrt(2.0 / n) * np.sin(2 * np.pi * ((m * j) % n) / n))
    return np.stack(rows)


def tables():
    q = real_basis()
    forward_z = np.zeros((4, 256, 256))
    inverse_z = np.zeros((4, 256, 256))
    for r in range(4):
        forward_z[r, 32 * r : 32 * r + SIDE, :SIDE] = q.T
        inverse_z[r, :SIDE, 32 * r : 32 * r + SIDE] = q
    order = np.array([4 * g + r for r in range(4) for g in range(GROUPS)])
    forward_y = q[:, order]
    inverse_y = forward_y.T
    x_table = np.zeros((SIDE, 256))
    x_table[:, :SIDE] = q
    x_back = np.zeros((256, SIDE))
    x_back[:SIDE, :] = q.T
    return [halves(t) for t in (forward_z, forward_y, inverse_y, inverse_z, x_table, x_back)]


def split(value):
    high = value.astype(bf16)
    low = (value - high.astype(f32)).astype(bf16)
    return high, low


def dot(a, b):
    return jnp.dot(a, b, preferred_element_type=f32)


def dot3(a, b):
    return dot(a[0], b[0]) + (dot(a[0], b[1]) + dot(a[1], b[0]))


def kernel(
    starts, occ, orb_hbm, pot_hbm, bg_hbm, fz_hbm, fy_hbm, iy_hbm, iz_hbm, xt_hbm, xb_hbm,
    psi_out, field_out,
    raw, pot, bg, fz, fy, iy, iz, xt, xb,
    cur, psi, diag, half, ion,
    send_lo, send_hi, halo_lo, halo_hi,
    rho_own, rho_rx, rho_chip, rho_y, xc,
    za, zb, e_rho, e_ion, recv_rho, recv_ion, result, spec, hsc, field,
    load_sem, table_sem, out_sem,
    send_lo_sem, send_hi_sem, recv_lo_sem, recv_hi_sem,
    part_send, part_recv, y_send, y_recv, xc_send, xc_recv,
    fwd_send, rho_recv, ion_send, ion_recv, back_send, back_recv, mid_send, mid_recv,
    ready_a, ready_b,
):
    s = lax.axis_index("state")
    d = lax.axis_index("domain")
    core = s % 2
    ylo = s // 2
    chip = d * 2 + ylo

    def dev(state, domain):
        return {"state": state, "domain": domain}

    partner = dev(ylo * 2 + 1 - core, d)
    across = dev((1 - ylo) * 2 + core, d)
    has_low = d > 0
    has_high = d < DOMAINS - 1
    low_dev = dev(s, jnp.maximum(d - 1, 0))
    high_dev = dev(s, jnp.minimum(d + 1, DOMAINS - 1))
    octet = d // 8
    place = d % 8

    barrier = pltpu.get_barrier_semaphore()

    def greet(state, domain):
        pl.semaphore_signal(barrier, inc=1, device_id=dev(state, domain), device_id_type=MESH)

    for step in range(1, 8):
        greet(s, octet * 8 + (place + step) % 8)
    for step in range(1, 4):
        greet((s + step) % 4, d)
        greet(s, (d + 8 * step) % DOMAINS)
    cross_low = jnp.logical_and(place == 0, has_low)
    cross_high = jnp.logical_and(place == 7, has_high)

    @pl.when(cross_low)
    def _():
        greet(s, jnp.maximum(d - 1, 0))

    @pl.when(cross_high)
    def _():
        greet(s, jnp.minimum(d + 1, DOMAINS - 1))

    def loads(ch):
        lanes = pl.ds(ch * (CHUNK_GROUPS * LANES), CHUNK_GROUPS * LANES)
        return (
            pltpu.make_async_copy(orb_hbm.at[:, :, lanes], raw.at[:, :, lanes], load_sem.at[0, ch]),
            pltpu.make_async_copy(pot_hbm.at[:, lanes], pot.at[:, lanes], load_sem.at[1, ch]),
            pltpu.make_async_copy(bg_hbm.at[:, lanes], bg.at[:, lanes], load_sem.at[2, ch]),
        )

    for ch in range(CHUNKS):
        for copy in loads(ch):
            copy.start()
    table_copies = [
        pltpu.make_async_copy(src, dst, table_sem.at[i])
        for i, (src, dst) in enumerate(
            ((fz_hbm, fz), (fy_hbm, fy), (iy_hbm, iy), (iz_hbm, iz), (xt_hbm, xt), (xb_hbm, xb))
        )
    ]
    for copy in table_copies:
        copy.start()

    own_start = starts[d]
    thickness = starts[d + 1] - own_start
    top_row = jnp.clip(thickness - 1, 0, LAYERS - 1)
    lane = lax.broadcasted_iota(i32, (8, LANES), 1)
    sub = lax.broadcasted_iota(i32, (8, LANES), 0)
    y_low = (
        (lane >= SIDE).astype(i32) + (lane >= 2 * SIDE).astype(i32) + (lane >= 3 * SIDE).astype(i32)
    )
    z_off = (2 * (lane - SIDE * y_low) - (SIDE - 1)).astype(f32)
    z_square = z_off * z_off
    y_base = (2 * y_low - (SIDE - 1)).astype(f32)
    x_off = (2 * (own_start + sub) - (SIDE - 1)).astype(f32)
    xz_square = jnp.where(sub < thickness, x_off * x_off, 1.0e9) + z_square
    radius = float((SIDE - 2) ** 2)
    is_low = sub == 0
    is_high = sub == top_row

    def mask_of(g):
        y_off = y_base + (8 * g).astype(f32)
        return jnp.where(y_off * y_off + xz_square <= radius, 1.0, 0.0)

    def lanes_of(g):
        return pl.ds(pl.multiple_of(g * LANES, 128), LANES)

    def edge_sends(k, ch):
        to_low = pltpu.make_async_remote_copy(
            send_lo.at[k, ch], halo_hi.at[k, ch], send_lo_sem.at[k, ch], recv_hi_sem.at[k, ch],
            device_id=low_dev, device_id_type=MESH,
        )
        to_high = pltpu.make_async_remote_copy(
            send_hi.at[k, ch], halo_lo.at[k, ch], send_hi_sem.at[k, ch], recv_lo_sem.at[k, ch],
            device_id=high_dev, device_id_type=MESH,
        )
        return to_low, to_high

    def start_edges(k, ch):
        to_low, to_high = edge_sends(k, ch)

        @pl.when(has_low)
        def _():
            to_low.start()

        @pl.when(has_high)
        def _():
            to_high.start()

    def await_edges(k, ch):
        to_low, to_high = edge_sends(k, ch)

        @pl.when(has_low)
        def _():
            to_high.wait_recv()

        @pl.when(has_high)
        def _():
            to_low.wait_recv()

    zero_group = jnp.zeros((8, LANES), f32)
    for which in range(2):
        for c in range(2):
            cur[which, c, 0] = zero_group
            cur[which, c, GROUPS + 1] = zero_group

    @pl.when(jnp.logical_not(has_low))
    def _():
        halo_lo[...] = jnp.zeros(halo_lo.shape, f32)

    @pl.when(jnp.logical_not(has_high))
    def _():
        halo_hi[...] = jnp.zeros(halo_hi.shape, f32)

    pl.semaphore_wait(
        barrier, 13 + jnp.where(cross_low, 1, 0) + jnp.where(cross_high, 1, 0)
    )

    for ch in range(CHUNKS):
        copies = loads(ch)
        copies[0].wait()
        copies[1].wait()

        def first(gi, carry, ch=ch):
            g = ch * CHUNK_GROUPS + gi
            mask = mask_of(g)
            lanes = lanes_of(g)
            diag[g] = zero_group
            half[g] = 0.5 * mask
            diag[g, 0:7, :] = (3.0 + pot[:, lanes]) * mask[0:7, :]
            for c in range(2):
                value = raw[c, :, lanes] * mask[0:7, :]
                cur[0, c, g + 1] = zero_group
                cur[0, c, g + 1, 0:7, :] = value
                psi[c, g] = zero_group
                psi[c, g, 0:7, :] = value
                send_lo[0, ch, c, pl.ds(gi, 1), :] = value[0:1, :]
                send_hi[0, ch, c, pl.ds(gi, 1), :] = cur[0, c, g + 1, pl.ds(top_row, 1), :]
            return carry

        lax.fori_loop(0, CHUNK_GROUPS, first, 0)
        start_edges(0, ch)

    for step in range(1, 4):
        pl.semaphore_signal(ready_a, inc=1, device_id=dev((s + step) % 4, d), device_id_type=MESH)

    def beside(src, c, g, k, ch, gi):
        own = cur[src, c, g + 1]
        before = cur[src, c, g, :, 384:640]
        after = cur[src, c, g + 2, :, 0:256]
        wide = jnp.concatenate([before, own, after], axis=1)
        total = 1152
        shifted = (
            pltpu.roll(wide, 1, 1)
            + pltpu.roll(wide, total - 1, 1)
            + pltpu.roll(wide, SIDE, 1)
            + pltpu.roll(wide, total - SIDE, 1)
        )[:, 256:896]
        low = jnp.broadcast_to(halo_lo[k, ch, c, pl.ds(gi, 1), :], (8, LANES))
        high = jnp.broadcast_to(halo_hi[k, ch, c, pl.ds(gi, 1), :], (8, LANES))
        rim = jnp.where(is_low, low, jnp.where(is_high, high, 0.0))
        stacked = pltpu.roll(own, 1, 0) + pltpu.roll(own, 7, 0)
        return own, shifted + (stacked + rim)

    def taylor(k):
        factor = time_step / k
        src, dst = (k - 1) % 2, k % 2

        def chunk(ch, carry):
            await_edges(k - 1, ch)

            def group(gi, inner):
                g = ch * CHUNK_GROUPS + gi
                diagonal = diag[g]
                weight = half[g]
                applied = []
                for c in range(2):
                    own, around = beside(src, c, g, k - 1, ch, gi)
                    applied.append(diagonal * own - weight * around)
                fresh = (factor * applied[1], -factor * applied[0])
                if k < TERMS:
                    for c in range(2):
                        cur[dst, c, g + 1] = fresh[c]
                        psi[c, g] = psi[c, g] + fresh[c]
                        send_lo[k, ch, c, pl.ds(gi, 1), :] = fresh[c][0:1, :]
                        send_hi[k, ch, c, pl.ds(gi, 1), :] = cur[
                            dst, c, g + 1, pl.ds(top_row, 1), :
                        ]
                else:
                    lanes = lanes_of(g)
                    squares = zero_group
                    for c in range(2):
                        value = psi[c, g] + fresh[c]
                        field_psi = value[0:7, :]
                        raw[c, :, lanes] = field_psi
                        squares = squares + value * value
                    rho_own[g] = occ[0] * squares
                return inner

            lax.fori_loop(0, CHUNK_GROUPS, group, 0)
            if k < TERMS:
                start_edges(k, ch)
            else:
                share_rho(ch).start()
            return carry

        lax.fori_loop(0, CHUNKS, chunk, 0)

    def share_rho(ch):
        rows = pl.ds(ch * CHUNK_GROUPS, CHUNK_GROUPS)
        return pltpu.make_async_remote_copy(
            rho_own.at[rows], rho_rx.at[rows], part_send.at[ch], part_recv.at[ch],
            device_id=partner, device_id_type=MESH,
        )

    def forward_z(src):
        for r in range(4):
            left = src[:, :, 128 * r : 128 * r + 256].reshape(GROUPS * 8, 256)
            out = dot3(split(left), (fz[0, r], fz[1, r]))
            za[r * 320 : (r + 1) * 320, :] = out[:, 0:128]
            zb[r * 320 : (r + 1) * 320, :] = out[:, 128:256]

    def forward_y(dst, slots):
        for slot in slots:
            rows = pl.ds(slot, SIDE, stride=8)
            right = jnp.concatenate([za[rows, :], zb[rows, :]], axis=1)
            out = dot3((fy[0], fy[1]), split(right))
            dst[rows, :] = out[:, 0:128]
            tail = out[:, 128:256]
            packed = tail[0:40, :]
            for j in range(1, 4):
                packed = packed + pltpu.roll(tail[40 * j : 40 * j + 40, :], 32 * j, 1)
            dst[pl.ds(SIDE * 8 + slot, 40, stride=8), :] = packed

    def put_total(dst, partial):
        total = jnp.broadcast_to(jnp.sum(partial, axis=0, keepdims=True), (200, 128))
        dst[pl.ds(7, 200, stride=8), :] = total

    def fold(value):
        part = value[:, 0:128]
        for j in range(1, 5):
            part = part + value[:, 128 * j : 128 * j + 128]
        return part

    taylor(1)

    for ch in range(CHUNKS):
        loads(ch)[2].wait()

    def ion_group(g, acc):
        ion[g] = zero_group
        value = bg[:, lanes_of(g)] * (2.0 * half[g, 0:7, :])
        ion[g, 0:7, :] = value
        return acc + fold(ion[g])

    ion_total = lax.fori_loop(0, GROUPS, ion_group, jnp.zeros((8, 128), f32))
    for copy in table_copies:
        copy.wait()
    forward_z(ion)

    taylor(2)
    forward_y(e_ion, range(0, 4))

    pl.semaphore_wait(ready_a, 3)
    for step in range(1, 4):
        pl.semaphore_signal(
            ready_b, inc=1, device_id=dev(s, (d + 8 * step) % DOMAINS), device_id_type=MESH
        )

    taylor(3)
    forward_y(e_ion, range(4, 7))
    put_total(e_ion, ion_total)
    pl.semaphore_wait(ready_b, 3)

    other = 1 - core

    def owner_dev(p):
        place_of = (p * 32) // 25
        return dev((place_of % 2) * 2 + other, place_of // 2)

    def column_rows(p, half_of):
        return pl.ds(pl.multiple_of((2 * p + half_of) * 16, 16), 16)

    def send_ion(j):
        p = 2 * ((j + d) % 25) + ylo
        return pltpu.make_async_remote_copy(
            e_ion.at[column_rows(p, other), :],
            recv_ion.at[pl.ds(pl.multiple_of(d * 16, 16), 16), :],
            ion_send, ion_recv, device_id=owner_dev(p), device_id_type=MESH,
        )

    def send_rho(j):
        p = (j + (chip * 25) // 32) % PAIRS
        return pltpu.make_async_remote_copy(
            e_rho.at[column_rows(p, other), :],
            recv_rho.at[pl.ds(pl.multiple_of((ylo * DOMAINS + d) * 16, 16), 16), :],
            fwd_send, rho_recv, device_id=owner_dev(p), device_id_type=MESH,
        )

    def start_all(make, count):
        def one(j, carry):
            make(j).start()
            return carry

        lax.fori_loop(0, count, one, 0)

    start_all(send_ion, 25)

    taylor(4)
    psi_copy = pltpu.make_async_copy(raw, psi_out, out_sem.at[0])
    psi_copy.start()

    def chip_sum(ch, acc):
        share_rho(ch).wait_recv()

        def group(gi, inner):
            g = ch * CHUNK_GROUPS + gi
            value = rho_own[g] + rho_rx[g]
            rho_chip[g] = value
            return inner + fold(value)

        return lax.fori_loop(0, CHUNK_GROUPS, group, acc)

    rho_total = lax.fori_loop(0, CHUNKS, chip_sum, jnp.zeros((8, 128), f32))

    forward_z(rho_chip)
    forward_y(e_rho, range(7))
    put_total(e_rho, rho_total)
    start_all(send_rho, PAIRS)

    half_rows = pl.ds(pl.multiple_of(core * 20, 4), 20)
    y_copy = pltpu.make_async_remote_copy(
        rho_chip.at[half_rows], rho_y, y_send, y_recv, device_id=across, device_id_type=MESH
    )
    y_copy.start()

    pair_of = (chip * 25 + 31) // 32
    is_owner = jnp.logical_and((pair_of * 32) // 25 == chip, pair_of < PAIRS)

    def await_bytes(ref, sem):
        pltpu.make_async_copy(ref, ref, sem).wait()

    def send_back(j):
        q = (j + chip) % CHIPS
        return pltpu.make_async_remote_copy(
            result.at[pl.ds(pl.multiple_of((q // 2) * 16, 16), 16), :],
            spec.at[pl.ds(pl.multiple_of((2 * pair_of + core) * 16, 16), 16), :],
            back_send, back_recv,
            device_id=dev((q % 2) * 2 + other, q // 2), device_id_type=MESH,
        )

    @pl.when(is_owner)
    def _():
        lane256 = lax.broadcasted_iota(i32, (SIDE, 256), 1)
        row160 = lax.broadcasted_iota(i32, (SIDE, 256), 0)
        lane_row = lax.broadcasted_iota(i32, (8, 256), 1)
        slot_row = lane_row % 8
        dom_row = lane_row // 8
        where_x = jnp.full((8, 256), -1, i32)
        pieces = []
        sub256 = lax.broadcasted_iota(i32, (8, 256), 0)
        for k in range(DOMAINS):
            first_x = starts[k]
            count = starts[k + 1] - first_x
            where_x = jnp.where(
                jnp.logical_and(dom_row == k, slot_row < count), first_x + slot_row, where_x
            )
            hit = jnp.logical_and(lane_row == first_x + sub256, sub256 < count)
            pieces.append(jnp.where(hit, 1.0, 0.0))
        select_back = jnp.concatenate(pieces, axis=0).astype(bf16)
        wide_x = jnp.broadcast_to(where_x[0:1, :], (256, 256))
        row256 = lax.broadcasted_iota(i32, (256, 256), 0)
        select = jnp.where(wide_x == row256, 1.0, 0.0).astype(bf16)
        x_fwd = (dot(xt[0], select).astype(bf16), dot(xt[1], select).astype(bf16))
        x_inv = (dot(select_back, xb[0]).astype(bf16), dot(select_back, xb[1]).astype(bf16))
        o = 2 * pair_of + core
        unit = 2 * o + lane256 // 128
        low_lane = lane256 % 128
        is_tail = unit >= SIDE
        ky = jnp.where(is_tail, 40 * (low_lane // 32) + unit - SIDE, unit)
        kz = jnp.where(is_tail, 128 + low_lane % 32, low_lane)

        def wave(index):
            folded = jnp.where(2 * index <= SIDE, index, index - SIDE // 2)
            number = folded.astype(f32) * (two_pi / SIDE)
            return number * number

        squared = wave(row160) + wave(ky) + wave(kz)
        coulomb = jnp.where(squared > 0, four_pi / jnp.where(squared > 0, squared, 1.0), 0.0)

        await_bytes(recv_ion, ion_recv)
        await_bytes(recv_rho, rho_recv)
        ions = recv_ion[...].reshape(DOMAINS, 2, 8, 128)
        dens = recv_rho[...].reshape(2, DOMAINS, 2, 8, 128)
        dens = dens[0] + dens[1]
        sub8 = lax.broadcasted_iota(i32, (8, 128), 0)

        def total_of(array):
            rows = jnp.sum(array[:, 0], axis=0)
            return jnp.sum(jnp.where(sub8 == 7, rows, 0.0), axis=(0, 1), keepdims=True)

        scale = total_of(dens) / total_of(ions)
        charge = dens - scale.reshape(1, 1, 1, 1) * ions
        right = jnp.concatenate(
            [charge[:, 0].reshape(256, 128), charge[:, 1].reshape(256, 128)], axis=1
        )
        waves = dot3(x_fwd, split(right)) * coulomb
        back = dot3(x_inv, split(waves))
        result[...] = jnp.stack(
            [back[:, 0:128].reshape(DOMAINS, 8, 128), back[:, 128:256].reshape(DOMAINS, 8, 128)],
            axis=1,
        ).reshape(DOMAINS * 16, 128)
        start_all(send_back, CHIPS)

    y_copy.wait_recv()

    def root(i, carry):
        value = (3.0 / math.pi) * (rho_chip[core * 20 + i] + rho_y[i])
        positive = value > 1.0e-37
        safe = jnp.where(positive, value, 1.0)
        guess = jnp.exp(jnp.log(safe) * (1.0 / 3.0))
        guess = (2.0 * guess + safe / (guess * guess)) * (1.0 / 3.0)
        xc[core * 20 + i] = jnp.where(positive, guess, 0.0)
        return carry

    lax.fori_loop(0, 20, root, 0)
    xc_copy = pltpu.make_async_remote_copy(
        xc.at[half_rows], xc.at[half_rows], xc_send, xc_recv,
        device_id=partner, device_id_type=MESH,
    )
    xc_copy.start()

    await_bytes(spec.at[pl.ds(0, 800), :], back_recv)

    def swap(p):
        rows = column_rows(p, other)
        return pltpu.make_async_remote_copy(
            spec.at[rows, :], spec.at[rows, :], mid_send, mid_recv,
            device_id=partner, device_id_type=MESH,
        )

    start_all(swap, PAIRS)
    await_bytes(spec.at[pl.ds(0, 800), :], mid_recv)

    for slot in range(7):
        rows = pl.ds(slot, SIDE, stride=8)
        main = spec[rows, :]
        tail = spec[pl.ds(SIDE * 8 + slot, 40, stride=8), :]
        parts = [tail] + [pltpu.roll(tail, 128 - 32 * j, 1) for j in range(1, 4)]
        right = jnp.concatenate([main, jnp.concatenate(parts, axis=0)], axis=1)
        out = dot3((iy[0], iy[1]), split(right))
        za[rows, :] = out[:, 0:128]
        zb[rows, :] = out[:, 128:256]
    carried = None
    for r in range(4):
        left = jnp.concatenate(
            [za[r * 320 : (r + 1) * 320, :], zb[r * 320 : (r + 1) * 320, :]], axis=1
        )
        out = dot3(split(left), (iz[0, r], iz[1, r]))
        piece = out[:, 0:128]
        if carried is not None:
            piece = piece + carried
        hsc[:, :, 128 * r : 128 * r + 128] = piece.reshape(GROUPS, 8, 128)
        carried = out[:, 128:256]
    hsc[:, :, 512:640] = carried.reshape(GROUPS, 8, 128)

    xc_copy.wait_recv()

    def finish(g, carry):
        value = (hsc[g] - xc[g]) * (2.0 * half[g])
        value = jnp.where(half[g] > 0.0, value, 0.0)
        field[:, lanes_of(g)] = value[0:7, :]
        return carry

    lax.fori_loop(0, GROUPS, finish, 0)
    field_copy = pltpu.make_async_copy(field, field_out, out_sem.at[1])
    field_copy.start()

    for k in range(TERMS):
        def drain(ch, carry, k=k):
            to_low, to_high = edge_sends(k, ch)

            @pl.when(has_low)
            def _():
                to_low.wait_send()

            @pl.when(has_high)
            def _():
                to_high.wait_send()

            return carry

        lax.fori_loop(0, CHUNKS, drain, 0)

    def drain_rho(ch, carry):
        share_rho(ch).wait_send()
        return carry

    lax.fori_loop(0, CHUNKS, drain_rho, 0)
    y_copy.wait_send()
    xc_copy.wait_send()
    await_bytes(e_ion.at[pl.ds(0, 400), :], ion_send)
    await_bytes(e_rho.at[pl.ds(0, 800), :], fwd_send)
    await_bytes(spec.at[pl.ds(0, 800), :], mid_send)

    @pl.when(is_owner)
    def _():
        await_bytes(recv_rho, back_send)

    psi_copy.wait()
    field_copy.wait()


def step(orbitals, occupation, potential, background, layer_start):
    tabs = [jnp.asarray(t) for t in tables()]
    vmem = lambda *shape: pltpu.VMEM(shape, f32)
    dma = pltpu.SemaphoreType.DMA
    anyspace = pl.BlockSpec(memory_space=pl.ANY)
    smem = pl.BlockSpec(memory_space=pltpu.SMEM)
    wide = CHUNK_GROUPS * LANES
    edge = (TERMS, CHUNKS, 2, CHUNK_GROUPS, LANES)
    cube = (GROUPS, 8, LANES)
    columns = (1600, 128)
    scratch = [
        vmem(2, LAYERS, PLANE), vmem(LAYERS, PLANE), vmem(LAYERS, PLANE),
        *[pltpu.VMEM(t.shape, bf16) for t in tabs],
        vmem(2, 2, GROUPS + 2, 8, LANES), vmem(2, *cube), vmem(*cube), vmem(*cube), vmem(*cube),
        vmem(*edge), vmem(*edge), vmem(*edge), vmem(*edge),
        vmem(*cube), vmem(*cube), vmem(*cube), vmem(20, 8, LANES), vmem(*cube),
        vmem(1280, 128), vmem(1280, 128), vmem(*columns), vmem(*columns),
        vmem(1024, 128), vmem(512, 128), vmem(512, 128), vmem(*columns),
        vmem(*cube), vmem(LAYERS, PLANE),
        dma((3, CHUNKS)), dma((6,)), dma((2,)),
        dma((TERMS, CHUNKS)), dma((TERMS, CHUNKS)), dma((TERMS, CHUNKS)), dma((TERMS, CHUNKS)),
        dma((CHUNKS,)), dma((CHUNKS,)),
        *[dma(()) for _ in range(12)],
        pltpu.SemaphoreType.REGULAR, pltpu.SemaphoreType.REGULAR,
    ]
    psi, field = pl.pallas_call(
        kernel,
        out_shape=(
            jax.ShapeDtypeStruct((2, LAYERS, PLANE), f32),
            jax.ShapeDtypeStruct((LAYERS, PLANE), f32),
        ),
        in_specs=[smem, smem] + [anyspace] * 9,
        out_specs=(anyspace, anyspace),
        scratch_shapes=scratch,
        compiler_params=pltpu.CompilerParams(
            collective_id=0, has_side_effects=True, vmem_limit_bytes=60 * 1024 * 1024
        ),
    )(
        layer_start, occupation, orbitals.reshape(2, LAYERS, PLANE), potential, background, *tabs
    )
    return psi.reshape(2, 1, LAYERS, PLANE), field


def solution(mesh):
    return jax.shard_map(
        step,
        mesh=mesh,
        in_specs=(
            P(None, "state", "domain", None),
            P("state"),
            P("domain", None),
            P("domain", None),
            P(),
        ),
        out_specs=(P(None, "state", "domain", None), P("domain", None)),
        check_vma=False,
    )
```

```python
import functools
import math

import jax
import jax.numpy as jnp
import numpy as np
from jax import lax
from jax.experimental import pallas as pl
from jax.experimental.pallas import tpu as pltpu
from jax.sharding import PartitionSpec as P

SIDE = 160
SLAB = 5
TERMS = 4
LAYERS = 7
PLANE = SIDE * SIDE
GROUPS = 40
LANES = 640
CHUNKS = 5
CHUNK_GROUPS = 8
OWNERS = 100
PAIRS = 50
DOMAINS = 32
STATES = 4
CHIPS = 64

time_step = 0.3
four_pi = 4.0 * math.pi
two_pi = 2.0 * math.pi
MESH = pl.DeviceIdType.MESH
f32 = jnp.float32
i32 = jnp.int32
bf16 = jnp.bfloat16


def halves(table):
    table = np.asarray(table, np.float32)
    high = table.astype(bf16)
    low = (table - high.astype(np.float32)).astype(bf16)
    return np.stack([high, low])


def real_basis():
    n = SIDE
    j = np.arange(n)
    rows = []
    for i in range(n):
        if i == 0:
            rows.append(np.full(n, math.sqrt(1.0 / n)))
        elif i < n // 2:
            rows.append(math.sqrt(2.0 / n) * np.cos(2 * np.pi * ((i * j) % n) / n))
        elif i == n // 2:
            rows.append(math.sqrt(1.0 / n) * np.where(j % 2 == 0, 1.0, -1.0))
        else:
            m = i - n // 2
            rows.append(math.sqrt(2.0 / n) * np.sin(2 * np.pi * ((m * j) % n) / n))
    return np.stack(rows)


def tables():
    q = real_basis()
    side_table = np.zeros((SIDE, 256))
    side_table[:, :SIDE] = q.T
    order = np.array([4 * g + r for r in range(4) for g in range(GROUPS)])
    forward_y = q[:, order]
    x_table = np.zeros((SIDE, 256))
    x_table[:, :SIDE] = q
    x_back = np.zeros((256, SIDE))
    x_back[:SIDE, :] = q.T
    half_y = np.zeros((2, 96, SIDE))
    for which in range(2):
        for j in range(4):
            for q in range(20):
                half_y[which, 24 * j + q] = forward_y[40 * j + 4 * (q // 2) + 2 * which + q % 2]
    high, low = halves(half_y)
    left_y = np.concatenate([high, high, low], axis=2)
    high, low = halves(forward_y.T)
    left_back = np.concatenate([high, high, low], axis=1)
    return [halves(side_table), left_y, left_back, halves(x_table), halves(x_back)]


def split(value):
    high = value.astype(bf16)
    low = (value - high.astype(f32)).astype(bf16)
    return high, low


def dot(a, b):
    return jnp.dot(a, b, preferred_element_type=f32)


def dot_t(a, b):
    dims = (((1,), (1,)), ((), ()))
    return lax.dot_general(a, b, dims, preferred_element_type=f32)


def stack_left(value, axis=1):
    high, low = split(value)
    return jnp.concatenate([high, high, low], axis=axis)


def stack_right(value, axis=0):
    high, low = split(value)
    return jnp.concatenate([high, low, high], axis=axis)


def kernel(
    starts, occ, orb_hbm, pot_hbm, bg_hbm, qz_hbm, fy_hbm, iy_hbm, xt_hbm, xb_hbm,
    psi_out, field_out,
    raw, pot, bg, qz, fy, iy, xt, xb, fz,
    cur_a, cur_b, psi, diag, half, ion,
    send_lo, send_hi, halo_lo, halo_hi,
    rho_own, rho_rx, rho_chip, rho_cols, rho_y, xc,
    za, zb, e_rho, e_ion, recv_rho, recv_ion, result, spec, hsc, field,
    x_fwd, x_inv, coulomb,
    load_sem, table_sem, out_sem,
    send_lo_sem, send_hi_sem, recv_lo_sem, recv_hi_sem,
    part_send, part_recv, y_send, y_recv, xc_send, xc_recv,
    fwd_send, rho_recv, ion_send, ion_recv, back_send, back_recv, mid_send, mid_recv,
    ready_a, ready_b,
):
    s = lax.axis_index("state")
    d = lax.axis_index("domain")
    core = s & 1
    ylo = s >> 1
    chip = d * 2 + ylo

    def dev(state, domain):
        return {"state": state, "domain": domain}

    partner = dev(ylo * 2 + 1 - core, d)
    across = dev((1 - ylo) * 2 + core, d)
    has_low = d > 0
    has_high = d < DOMAINS - 1
    low_dev = dev(s, jnp.maximum(d - 1, 0))
    high_dev = dev(s, jnp.minimum(d + 1, DOMAINS - 1))
    octet = d >> 3
    place = d & 7

    barrier = pltpu.get_barrier_semaphore()

    def greet(state, domain):
        pl.semaphore_signal(barrier, inc=1, device_id=dev(state, domain), device_id_type=MESH)

    for step in range(1, 8):
        greet(s, octet * 8 + ((place + step) & 7))
    for step in range(1, 4):
        greet((s + step) & 3, d)
        greet(s, (d + 8 * step) & (DOMAINS - 1))
    cross_low = jnp.logical_and(place == 0, has_low)
    cross_high = jnp.logical_and(place == 7, has_high)

    @pl.when(cross_low)
    def _():
        greet(s, jnp.maximum(d - 1, 0))

    @pl.when(cross_high)
    def _():
        greet(s, jnp.minimum(d + 1, DOMAINS - 1))

    orb_copy = pltpu.make_async_copy(orb_hbm, raw.at[pl.ds(0, 2800), :], load_sem.at[0])
    pot_copy = pltpu.make_async_copy(pot_hbm, pot, load_sem.at[1])
    bg_copy = pltpu.make_async_copy(bg_hbm, bg, load_sem.at[2])
    table_copies = [
        pltpu.make_async_copy(src, dst, table_sem.at[i])
        for i, (src, dst) in enumerate(
            ((qz_hbm, qz), (fy_hbm, fy), (iy_hbm, iy), (xt_hbm, xt), (xb_hbm, xb))
        )
    ]
    for copy in [orb_copy, pot_copy, bg_copy] + table_copies:
        copy.start()

    own_start = starts[d]
    thickness = starts[d + 1] - own_start
    top_row = jnp.clip(thickness - 1, 0, LAYERS - 1)
    lane = lax.broadcasted_iota(i32, (8, 128), 1)
    sub = lax.broadcasted_iota(i32, (8, 128), 0)
    radius = float((SIDE - 2) ** 2)
    x_off = (2 * (own_start + sub) - (SIDE - 1)).astype(f32)
    x_square = jnp.where(sub < thickness, x_off * x_off, 1.0e9)
    yz_parts = []
    for j in range(5):
        flat = lane + 128 * j
        y_low = (
            (flat >= SIDE).astype(i32)
            + (flat >= 2 * SIDE).astype(i32)
            + (flat >= 3 * SIDE).astype(i32)
        )
        z_off = (2 * (flat - SIDE * y_low) - (SIDE - 1)).astype(f32)
        yz_parts.append(((2 * y_low - (SIDE - 1)).astype(f32), x_square + z_off * z_off))
    is_spare = sub == 7
    is_above = sub == top_row + 1
    first_lane = lane == 0
    last_lane = lane == 127
    low_lanes = lane < 32
    high_lanes = lane >= 96

    def inside(g, j):
        y_base, xz_square = yz_parts[j]
        y_off = y_base + (8 * g).astype(f32)
        return y_off * y_off + xz_square <= radius

    def lanes_of(g, j):
        return pl.ds(pl.multiple_of(g * LANES + 128 * j, 128), 128)

    def rows_of(g):
        return pl.ds(pl.multiple_of(g * 8, 8), 8)

    def rows7_of(g):
        return pl.ds(pl.multiple_of(g * 8, 8), 7)

    def edge_sends(k, ch):
        to_low = pltpu.make_async_remote_copy(
            send_lo.at[k, ch], halo_hi.at[k, ch], send_lo_sem.at[k, ch], recv_hi_sem.at[k, ch],
            device_id=low_dev, device_id_type=MESH,
        )
        to_high = pltpu.make_async_remote_copy(
            send_hi.at[k, ch], halo_lo.at[k, ch], send_hi_sem.at[k, ch], recv_lo_sem.at[k, ch],
            device_id=high_dev, device_id_type=MESH,
        )
        return to_low, to_high

    def start_edges(k, ch):
        to_low, to_high = edge_sends(k, ch)

        @pl.when(has_low)
        def _():
            to_low.start()

        @pl.when(has_high)
        def _():
            to_high.start()

    def await_edges(k, ch):
        to_low, to_high = edge_sends(k, ch)

        @pl.when(has_low)
        def _():
            to_high.wait_recv()

        @pl.when(has_high)
        def _():
            to_low.wait_recv()

    zero = jnp.zeros((8, 128), f32)
    for cur in (cur_a, cur_b):
        for c in range(2):
            for j in range(5):
                cur[c, j, 0:8, :] = zero
                cur[c, j, 8 * GROUPS + 8 : 8 * GROUPS + 16, :] = zero

    def pick_edges(cur, k, ch):
        base = (ch * CHUNK_GROUPS + 1) * 8
        for c in range(2):
            for j in range(5):
                view = cur.at[c, j]
                send_lo[k, ch, c, j] = view[pl.ds(base, 8, stride=8), :]
                send_hi[k, ch, c, j] = view[pl.ds(base + top_row, 8, stride=8), :]

    @pl.when(jnp.logical_not(has_low))
    def _():
        halo_lo[...] = jnp.zeros(halo_lo.shape, f32)

    @pl.when(jnp.logical_not(has_high))
    def _():
        halo_hi[...] = jnp.zeros(halo_hi.shape, f32)

    orb_copy.wait()
    pot_copy.wait()

    def first_chunk(ch, carry):
        def first(gi, inner):
            for step_g in range(2):
                g = ch * CHUNK_GROUPS + gi * 2 + step_g
                for j in range(5):
                    keep = inside(g, j)
                    mask = jnp.where(keep, 1.0, 0.0)
                    half[j, rows_of(g), :] = 0.5 * mask
                    diag[j, rows_of(g), :] = zero
                    diag[j, rows7_of(g), :] = (3.0 + pot[:, lanes_of(g, j)]) * mask[0:7, :]
                    for c in range(2):
                        value = raw[pl.ds(c * 1400 + 5 * g + j, 8, stride=200), :]
                        value = jnp.where(keep, value, 0.0)
                        cur_a[c, j, rows_of(g + 1), :] = value
                        psi[c, j, rows_of(g), :] = value
            return inner

        lax.fori_loop(0, CHUNK_GROUPS // 2, first, 0)
        pick_edges(cur_a, 0, ch)
        return carry

    lax.fori_loop(0, CHUNKS, first_chunk, 0)
    pl.semaphore_wait(
        barrier, 13 + jnp.where(cross_low, 1, 0) + jnp.where(cross_high, 1, 0)
    )


    def send_first(ch, carry):
        start_edges(0, ch)
        return carry

    lax.fori_loop(0, CHUNKS, send_first, 0)

    for step in range(1, 4):
        pl.semaphore_signal(ready_a, inc=1, device_id=dev((s + step) & 3, d), device_id_type=MESH)

    span = 4

    def taylor(k):
        factor = time_step / k
        src, dst = (cur_a, cur_b) if k % 2 else (cur_b, cur_a)
        count = 5 * span

        def chunk(ch, carry):
            await_edges(k - 1, ch)

            def block(bi, inner):
                g0 = ch * CHUNK_GROUPS + bi * span

                def tile(c, v):
                    return src[c, v % 5, rows_of(g0 + 1 + v // 5), :]

                applied = []
                for c in range(2):
                    own = {v: tile(c, v) for v in range(-2, count + 2)}
                    right1 = {v: pltpu.roll(own[v], 1, 1) for v in range(-1, count)}
                    left1 = {v: pltpu.roll(own[v], 127, 1) for v in range(0, count + 1)}
                    right32 = {v: pltpu.roll(own[v], 32, 1) for v in range(-2, count - 0)}
                    left32 = {v: pltpu.roll(own[v], 96, 1) for v in range(1, count + 2)}
                    out = []
                    for v in range(count):
                        j, gi = v % 5, bi * span + v // 5
                        near = jnp.where(first_lane, right1[v - 1], right1[v]) + jnp.where(
                            last_lane, left1[v + 1], left1[v]
                        )
                        far = jnp.where(low_lanes, right32[v - 2], right32[v - 1]) + jnp.where(
                            high_lanes, left32[v + 2], left32[v + 1]
                        )
                        low = jnp.broadcast_to(
                            halo_lo[k - 1, ch, c, j, pl.ds(gi, 1), :], (8, 128)
                        )
                        high = jnp.broadcast_to(
                            halo_hi[k - 1, ch, c, j, pl.ds(gi, 1), :], (8, 128)
                        )
                        stacked = pltpu.roll(jnp.where(is_spare, low, own[v]), 1, 0) + pltpu.roll(
                            jnp.where(is_above, high, own[v]), 7, 0
                        )
                        rows = rows_of(g0 + v // 5)
                        out.append(
                            diag[j, rows, :] * own[v]
                            - half[j, rows, :] * ((near + far) + stacked)
                        )
                    applied.append(out)
                for v in range(count):
                    j = v % 5
                    g = g0 + v // 5
                    rows = rows_of(g)
                    fresh = (factor * applied[1][v], -factor * applied[0][v])
                    squares = zero
                    for c in range(2):
                        value = psi[c, j, rows, :] + fresh[c]
                        if k < TERMS:
                            dst[c, j, rows_of(g + 1), :] = fresh[c]
                            psi[c, j, rows, :] = value
                        else:
                            raw[pl.ds(c * 1400 + 5 * g + j, 7, stride=200), :] = value[0:7, :]
                            squares = squares + value * value
                    if k == TERMS:
                        rho_own[g, :, 128 * j : 128 * j + 128] = occ[0] * squares
                return inner

            lax.fori_loop(0, CHUNK_GROUPS // span, block, 0)
            if k < TERMS:
                pick_edges(dst, k, ch)
                start_edges(k, ch)
                return carry
            share_rho(ch).start()
            return chip_sum(ch - 1, ch > 0, carry)

        if k < TERMS:
            return lax.fori_loop(0, CHUNKS, chunk, 0)
        return chip_sum(CHUNKS - 1, None, lax.fori_loop(0, CHUNKS, chunk, zero))

    def chip_sum(ch, live, acc):
        if live is None:
            share_rho(ch).wait_recv()
        else:

            @pl.when(live)
            def _():
                share_rho(ch).wait_recv()

        def group(gi, inner):
            g = ch * CHUNK_GROUPS + gi
            for j in range(5):
                cols = slice(128 * j, 128 * j + 128)
                value = rho_own[g, :, cols] + rho_rx[g, :, cols]
                rho_chip[g, :, cols] = value
                rho_cols[j, rows_of(g), :] = value
                inner = inner + value
            return inner

        count = CHUNK_GROUPS if live is None else jnp.where(live, CHUNK_GROUPS, 0)
        return lax.fori_loop(0, count, group, acc)

    def share_rho(ch):
        rows = pl.ds(ch * CHUNK_GROUPS, CHUNK_GROUPS)
        return pltpu.make_async_remote_copy(
            rho_own.at[rows], rho_rx.at[rows], part_send.at[ch], part_recv.at[ch],
            device_id=partner, device_id_type=MESH,
        )

    def forward_z(src):
        parts = [split(src[j]) for j in range(5)]
        for r in range(4):
            high, low = (
                jnp.concatenate([parts[r][i], parts[r + 1][i]], axis=1) for i in range(2)
            )
            out = dot(jnp.concatenate([high, high, low], axis=1), fz[r])
            za[r * 320 : (r + 1) * 320, :] = out[:, 0:128]
            zb[r * 320 : (r + 1) * 320, :] = out[:, 128:256]

    other = 1 - core

    def forward_y(dst, slots):
        table = fy[other]
        for slot in slots:
            rows = pl.ds(slot, SIDE, stride=8)
            right = jnp.concatenate([za[rows, :], zb[rows, :]], axis=1)
            out = dot(table, stack_right(right))
            dst[pl.ds(slot, 96, stride=8), :] = out[:, 0:128]
            tail = out[:, 128:256]
            packed = tail[0:24, :]
            for j in range(1, 4):
                packed = packed + pltpu.roll(tail[24 * j : 24 * j + 24, :], 32 * j, 1)
            dst[pl.ds(96 * 8 + slot, 24, stride=8), :] = packed

    def put_total(dst, partial):
        total = jnp.broadcast_to(jnp.sum(partial, axis=0, keepdims=True), (120, 128))
        dst[pl.ds(7, 120, stride=8), :] = total

    pair_of = (chip * 25 + 31) >> 5
    is_owner = jnp.logical_and(lax.div(pair_of * 32, 25) == chip, pair_of < PAIRS)

    def build_x_tables():
        @pl.when(is_owner)
        def _():
            lane256 = lax.broadcasted_iota(i32, (SIDE, 256), 1)
            row160 = lax.broadcasted_iota(i32, (SIDE, 256), 0)
            lane_row = lax.broadcasted_iota(i32, (8, 256), 1)
            slot_row = lane_row % 8
            dom_row = lane_row // 8
            where_x = jnp.full((8, 256), -1, i32)
            pieces = []
            sub256 = lax.broadcasted_iota(i32, (8, 256), 0)
            for k in range(DOMAINS):
                first_x = starts[k]
                count = starts[k + 1] - first_x
                where_x = jnp.where(
                    jnp.logical_and(dom_row == k, slot_row < count), first_x + slot_row, where_x
                )
                hit = jnp.logical_and(lane_row == first_x + sub256, sub256 < count)
                pieces.append(jnp.where(hit, 1.0, 0.0))
            select_back = jnp.concatenate(pieces, axis=0).astype(bf16)
            wide_x = jnp.broadcast_to(where_x[0:1, :], (256, 256))
            row256 = lax.broadcasted_iota(i32, (256, 256), 0)
            select = jnp.where(wide_x == row256, 1.0, 0.0).astype(bf16)
            x_high, x_low = (dot(xt[i], select).astype(bf16) for i in range(2))
            x_fwd[...] = jnp.concatenate([x_high, x_high, x_low], axis=1)
            for i in range(2):
                x_inv[i] = dot(select_back, xb[i]).astype(bf16)
            o = 2 * pair_of + core
            unit = 2 * o + lane256 // 128
            low_lane = lane256 % 128
            is_tail = unit >= SIDE
            ky = jnp.where(is_tail, 40 * (low_lane // 32) + unit - SIDE, unit)
            kz = jnp.where(is_tail, 128 + low_lane % 32, low_lane)

            def wave(index):
                folded = jnp.where(2 * index <= SIDE, index, index - SIDE // 2)
                number = folded.astype(f32) * (two_pi / SIDE)
                return number * number

            squared = wave(row160) + wave(ky) + wave(kz)
            coulomb[...] = jnp.where(squared > 0, four_pi / jnp.where(squared > 0, squared, 1.0), 0.0)


    bg_copy.wait()

    def ion_group(g, acc):
        for j in range(5):
            weight = 2.0 * half[j, rows_of(g), :]
            ion[j, rows_of(g), :] = zero
            ion[j, rows7_of(g), :] = bg[:, lanes_of(g, j)] * weight[0:7, :]
            acc = acc + ion[j, rows_of(g), :]
        return acc

    ion_total = lax.fori_loop(0, GROUPS, ion_group, zero)
    for copy in table_copies:
        copy.wait()
    fz[...] = jnp.zeros(fz.shape, bf16)
    for i, which in enumerate((0, 1, 0)):
        for r in range(4):
            fz[r, 256 * i + 32 * r : 256 * i + 32 * r + SIDE, :] = qz[which]
    forward_z(ion)

    forward_y(e_ion, range(0, 4))
    taylor(1)
    forward_y(e_ion, range(4, 7))
    put_total(e_ion, ion_total)

    pl.semaphore_wait(ready_a, 3)
    for step in range(1, 4):
        pl.semaphore_signal(
            ready_b, inc=1, device_id=dev(s, (d + 8 * step) & (DOMAINS - 1)), device_id_type=MESH
        )

    taylor(2)
    build_x_tables()
    taylor(3)
    pl.semaphore_wait(ready_b, 3)

    def div(value, by):
        return lax.div(value, jnp.int32(by))

    def owner_dev(p):
        place_of = p + div(p * 7, 25)
        return dev((place_of & 1) * 2 + other, place_of >> 1)

    def sent_rows(p):
        tens = div(p, 10)
        return pl.ds(pl.multiple_of((4 * tens + 2 * p) * 8, 16), 16)

    def column_rows(p, half_of):
        return pl.ds(pl.multiple_of((2 * p + half_of) * 16, 16), 16)

    def wrap(value, count):
        return jnp.where(value >= count, value - count, value)

    ion_first = lax.rem(d, jnp.int32(25))
    rho_first = (chip * 25) >> 5

    def send_ion(j):
        p = 2 * wrap(j + ion_first, 25) + ylo
        return pltpu.make_async_remote_copy(
            e_ion.at[sent_rows(p), :],
            recv_ion.at[pl.ds(pl.multiple_of(d * 16, 16), 16), :],
            ion_send, ion_recv, device_id=owner_dev(p), device_id_type=MESH,
        )

    def send_rho(j):
        p = wrap(j + rho_first, PAIRS)
        return pltpu.make_async_remote_copy(
            e_rho.at[sent_rows(p), :],
            recv_rho.at[pl.ds(pl.multiple_of((ylo * DOMAINS + d) * 16, 16), 16), :],
            fwd_send, rho_recv, device_id=owner_dev(p), device_id_type=MESH,
        )

    def start_all(make, count):
        def one(j, carry):
            make(j).start()
            return carry

        lax.fori_loop(0, count, one, 0)

    start_all(send_ion, 25)

    rho_total = taylor(4)
    psi_copy = pltpu.make_async_copy(raw.at[pl.ds(0, 2800), :], psi_out, out_sem.at[0])
    psi_copy.start()

    forward_z(rho_cols)
    forward_y(e_rho, range(7))
    put_total(e_rho, rho_total)
    start_all(send_rho, PAIRS)

    half_rows = pl.ds(pl.multiple_of(core * 20, 4), 20)
    y_copy = pltpu.make_async_remote_copy(
        rho_chip.at[half_rows], rho_y, y_send, y_recv, device_id=across, device_id_type=MESH
    )
    y_copy.start()

    def await_bytes(ref, sem):
        pltpu.make_async_copy(ref, ref, sem).wait()

    def send_back(j):
        q = (j + chip) & (CHIPS - 1)
        return pltpu.make_async_remote_copy(
            result.at[pl.ds(pl.multiple_of((q >> 1) * 16, 16), 16), :],
            spec.at[pl.ds(pl.multiple_of((2 * pair_of + core) * 16, 16), 16), :],
            back_send, back_recv,
            device_id=dev((q & 1) * 2 + other, q >> 1), device_id_type=MESH,
        )

    @pl.when(is_owner)
    def _():
        await_bytes(recv_ion, ion_recv)
        await_bytes(recv_rho, rho_recv)
        ions = recv_ion[...].reshape(DOMAINS, 2, 8, 128)
        dens = recv_rho[...].reshape(2, DOMAINS, 2, 8, 128)
        dens = dens[0] + dens[1]
        sub8 = lax.broadcasted_iota(i32, (8, 128), 0)

        def total_of(array):
            rows = jnp.sum(array[:, 0], axis=0)
            return jnp.sum(jnp.where(sub8 == 7, rows, 0.0), axis=(0, 1), keepdims=True)

        scale = total_of(dens) / total_of(ions)
        charge = dens - scale.reshape(1, 1, 1, 1) * ions
        right = jnp.concatenate(
            [charge[:, 0].reshape(256, 128), charge[:, 1].reshape(256, 128)], axis=1
        )
        waves = dot(x_fwd[...], stack_right(right)) * coulomb[...]
        w_high, w_low = split(waves)
        back = dot(x_inv[0], w_high) + (dot(x_inv[0], w_low) + dot(x_inv[1], w_high))
        result[...] = jnp.stack(
            [back[:, 0:128].reshape(DOMAINS, 8, 128), back[:, 128:256].reshape(DOMAINS, 8, 128)],
            axis=1,
        ).reshape(DOMAINS * 16, 128)
        start_all(send_back, CHIPS)

    y_copy.wait_recv()

    def root(i, carry):
        value = (3.0 / math.pi) * (rho_chip[core * 20 + i] + rho_y[i])
        positive = value > 1.0e-37
        safe = jnp.where(positive, value, 1.0)
        guess = jnp.exp(jnp.log(safe) * (1.0 / 3.0))
        guess = (2.0 * guess + safe / (guess * guess)) * (1.0 / 3.0)
        xc[core * 20 + i] = jnp.where(positive, guess, 0.0)
        return carry

    lax.fori_loop(0, 20, root, 0)
    xc_copy = pltpu.make_async_remote_copy(
        xc.at[half_rows], xc.at[half_rows], xc_send, xc_recv,
        device_id=partner, device_id_type=MESH,
    )
    xc_copy.start()

    await_bytes(spec.at[pl.ds(0, 800), :], back_recv)

    def swap(p):
        rows = column_rows(p, other)
        return pltpu.make_async_remote_copy(
            spec.at[rows, :], spec.at[rows, :], mid_send, mid_recv,
            device_id=partner, device_id_type=MESH,
        )

    start_all(swap, PAIRS)
    await_bytes(spec.at[pl.ds(0, 800), :], mid_recv)

    for slot in range(7):
        rows = pl.ds(slot, SIDE, stride=8)
        main = spec[rows, :]
        tail = spec[pl.ds(SIDE * 8 + slot, 40, stride=8), :]
        parts = [tail] + [pltpu.roll(tail, 128 - 32 * j, 1) for j in range(1, 4)]
        right = jnp.concatenate([main, jnp.concatenate(parts, axis=0)], axis=1)
        out = dot(iy[...], stack_right(right))
        za[rows, :] = out[:, 0:128]
        zb[rows, :] = out[:, 128:256]
    carried = None
    for r in range(4):
        left = jnp.concatenate(
            [za[r * 320 : (r + 1) * 320, :], zb[r * 320 : (r + 1) * 320, :]], axis=1
        )
        high, low = split(left)
        out = dot_t(high, fz[r, 0:256, :] ) + dot_t(high, fz[r, 256:512, :])
        out = out + dot_t(low, fz[r, 0:256, :])
        piece = out[:, 0:128]
        if carried is not None:
            piece = piece + carried
        hsc[r] = piece
        carried = out[:, 128:256]
    hsc[4] = carried

    xc_copy.wait_recv()

    def finish(g, carry):
        for j in range(5):
            value = hsc[j, rows_of(g), :] - xc[g, :, 128 * j : 128 * j + 128]
            value = jnp.where(half[j, rows_of(g), :] > 0.0, value, 0.0)
            field[:, lanes_of(g, j)] = value[0:7, :]
        return carry

    lax.fori_loop(0, GROUPS, finish, 0)
    field_copy = pltpu.make_async_copy(field, field_out, out_sem.at[1])
    field_copy.start()

    for k in range(TERMS):
        def drain(ch, carry, k=k):
            to_low, to_high = edge_sends(k, ch)

            @pl.when(has_low)
            def _():
                to_low.wait_send()

            @pl.when(has_high)
            def _():
                to_high.wait_send()

            return carry

        lax.fori_loop(0, CHUNKS, drain, 0)

    def drain_rho(ch, carry):
        share_rho(ch).wait_send()
        return carry

    lax.fori_loop(0, CHUNKS, drain_rho, 0)
    y_copy.wait_send()
    xc_copy.wait_send()
    await_bytes(e_ion.at[pl.ds(0, 400), :], ion_send)
    await_bytes(e_rho.at[pl.ds(0, 800), :], fwd_send)
    await_bytes(spec.at[pl.ds(0, 800), :], mid_send)

    @pl.when(is_owner)
    def _():
        await_bytes(recv_rho, back_send)

    psi_copy.wait()
    field_copy.wait()


def step(orbitals, occupation, potential, background, layer_start):
    tabs = [jnp.asarray(t) for t in tables()]
    vmem = lambda *shape: pltpu.VMEM(shape, f32)
    dma = pltpu.SemaphoreType.DMA
    anyspace = pl.BlockSpec(memory_space=pl.ANY)
    smem = pl.BlockSpec(memory_space=pltpu.SMEM)
    edge = (TERMS, CHUNKS, 2, 5, CHUNK_GROUPS, 128)
    cube = (GROUPS, 8, LANES)
    columns = (1600, 128)
    tile5 = (5, 8 * GROUPS, 128)
    padded = (2, 5, 8 * GROUPS + 16, 128)
    scratch = [
        vmem(3000, 128), vmem(LAYERS, PLANE), vmem(LAYERS, PLANE),
        *[pltpu.VMEM(t.shape, bf16) for t in tabs],
        pltpu.VMEM((4, 768, 256), bf16),
        vmem(*padded), vmem(*padded), vmem(2, *tile5), vmem(*tile5), vmem(*tile5), vmem(*tile5),
        vmem(*edge), vmem(*edge), vmem(*edge), vmem(*edge),
        vmem(*cube), vmem(*cube), vmem(*cube), vmem(*tile5), vmem(20, 8, LANES), vmem(*cube),
        vmem(1280, 128), vmem(1280, 128), vmem(960, 128), vmem(960, 128),
        vmem(1024, 128), vmem(512, 128), vmem(512, 128), vmem(*columns),
        vmem(*tile5), vmem(LAYERS, PLANE),
        pltpu.VMEM((SIDE, 768), bf16), pltpu.VMEM((2, 256, SIDE), bf16), vmem(SIDE, 256),
        dma((3,)), dma((5,)), dma((2,)),
        dma((TERMS, CHUNKS)), dma((TERMS, CHUNKS)), dma((TERMS, CHUNKS)), dma((TERMS, CHUNKS)),
        dma((CHUNKS,)), dma((CHUNKS,)),
        *[dma(()) for _ in range(12)],
        pltpu.SemaphoreType.REGULAR, pltpu.SemaphoreType.REGULAR,
    ]
    psi, field = pl.pallas_call(
        kernel,
        out_shape=(
            jax.ShapeDtypeStruct((2800, 128), f32),
            jax.ShapeDtypeStruct((LAYERS, PLANE), f32),
        ),
        in_specs=[smem, smem] + [anyspace] * 8,
        out_specs=(anyspace, anyspace),
        scratch_shapes=scratch,
        compiler_params=pltpu.CompilerParams(
            collective_id=0, has_side_effects=True, vmem_limit_bytes=60 * 1024 * 1024
        ),
    )(
        layer_start, occupation, orbitals.reshape(2800, 128), potential, background, *tabs
    )
    return psi.reshape(2, 1, LAYERS, PLANE), field


def solution(mesh):
    return jax.shard_map(
        step,
        mesh=mesh,
        in_specs=(
            P(None, "state", "domain", None),
            P("state"),
            P("domain", None),
            P("domain", None),
            P(),
        ),
        out_specs=(P(None, "state", "domain", None), P("domain", None)),
        check_vma=False,
    )
```

```python
import functools
import math

import jax
import jax.numpy as jnp
import numpy as np
from jax import lax
from jax.experimental import pallas as pl
from jax.experimental.pallas import tpu as pltpu
from jax.sharding import PartitionSpec as P

SIDE = 160
SLAB = 5
TERMS = 4
LAYERS = 7
PLANE = SIDE * SIDE
GROUPS = 40
LANES = 640
CHUNKS = 10
CHUNK_GROUPS = 4
OWNERS = 100
PAIRS = 50
DOMAINS = 32
STATES = 4
CHIPS = 64

time_step = 0.3
four_pi = 4.0 * math.pi
two_pi = 2.0 * math.pi
MESH = pl.DeviceIdType.MESH
f32 = jnp.float32
i32 = jnp.int32
bf16 = jnp.bfloat16


def halves(table):
    table = np.asarray(table, np.float32)
    high = table.astype(bf16)
    low = (table - high.astype(np.float32)).astype(bf16)
    return np.stack([high, low])


def real_basis():
    n = SIDE
    j = np.arange(n)
    rows = []
    for i in range(n):
        if i == 0:
            rows.append(np.full(n, math.sqrt(1.0 / n)))
        elif i < n // 2:
            rows.append(math.sqrt(2.0 / n) * np.cos(2 * np.pi * ((i * j) % n) / n))
        elif i == n // 2:
            rows.append(math.sqrt(1.0 / n) * np.where(j % 2 == 0, 1.0, -1.0))
        else:
            m = i - n // 2
            rows.append(math.sqrt(2.0 / n) * np.sin(2 * np.pi * ((m * j) % n) / n))
    return np.stack(rows)


def tables():
    q = real_basis()
    side_table = np.zeros((SIDE, 256))
    side_table[:, :SIDE] = q.T
    order = np.array([4 * g + r for r in range(4) for g in range(GROUPS)])
    forward_y = q[:, order]
    x_table = np.zeros((SIDE, 256))
    x_table[:, :SIDE] = q
    x_back = np.zeros((256, SIDE))
    x_back[:SIDE, :] = q.T
    half_y = np.zeros((2, 96, SIDE))
    for which in range(2):
        for j in range(4):
            for q in range(20):
                half_y[which, 24 * j + q] = forward_y[40 * j + 4 * (q // 2) + 2 * which + q % 2]
    high, low = halves(half_y)
    left_y = np.concatenate([high, high, low], axis=2)
    high, low = halves(forward_y.T)
    left_back = np.concatenate([high, high, low], axis=1)
    return [halves(side_table), left_y, left_back, halves(x_table), halves(x_back)]


def split(value):
    high = value.astype(bf16)
    low = (value - high.astype(f32)).astype(bf16)
    return high, low


def dot(a, b):
    return jnp.dot(a, b, preferred_element_type=f32)


def dot_t(a, b):
    dims = (((1,), (1,)), ((), ()))
    return lax.dot_general(a, b, dims, preferred_element_type=f32)


def stack_left(value, axis=1):
    high, low = split(value)
    return jnp.concatenate([high, high, low], axis=axis)


def stack_right(value, axis=0):
    high, low = split(value)
    return jnp.concatenate([high, low, high], axis=axis)


def kernel(
    starts, occ, orb_hbm, pot_hbm, bg_hbm, qz_hbm, fy_hbm, iy_hbm, xt_hbm, xb_hbm,
    psi_out, field_out,
    raw, pot, bg, qz, fy, iy, xt, xb, fz,
    cur_a, cur_b, psi, diag, half, ion,
    send_lo, send_hi, halo_lo, halo_hi,
    rho_own, rho_rx, rho_chip, rho_cols, rho_y, xc,
    za, zb, e_rho, e_ion, recv_rho, recv_ion, result, spec, hsc, field,
    x_fwd, x_inv, coulomb,
    load_sem, table_sem, out_sem,
    send_lo_sem, send_hi_sem, recv_lo_sem, recv_hi_sem,
    part_send, part_recv, y_send, y_recv, xc_send, xc_recv,
    fwd_send, rho_recv, ion_send, ion_recv, back_send, back_recv, mid_send, mid_recv,
    ready_a, ready_b,
):
    s = lax.axis_index("state")
    d = lax.axis_index("domain")
    core = s & 1
    ylo = s >> 1
    chip = d * 2 + ylo

    def dev(state, domain):
        return {"state": state, "domain": domain}

    partner = dev(ylo * 2 + 1 - core, d)
    across = dev((1 - ylo) * 2 + core, d)
    has_low = d > 0
    has_high = d < DOMAINS - 1
    low_dev = dev(s, jnp.maximum(d - 1, 0))
    high_dev = dev(s, jnp.minimum(d + 1, DOMAINS - 1))
    octet = d >> 3
    place = d & 7

    barrier = pltpu.get_barrier_semaphore()

    def greet(state, domain):
        pl.semaphore_signal(barrier, inc=1, device_id=dev(state, domain), device_id_type=MESH)

    for step in range(1, 8):
        greet(s, octet * 8 + ((place + step) & 7))
    for step in range(1, 4):
        greet((s + step) & 3, d)
        greet(s, (d + 8 * step) & (DOMAINS - 1))
    cross_low = jnp.logical_and(place == 0, has_low)
    cross_high = jnp.logical_and(place == 7, has_high)

    @pl.when(cross_low)
    def _():
        greet(s, jnp.maximum(d - 1, 0))

    @pl.when(cross_high)
    def _():
        greet(s, jnp.minimum(d + 1, DOMAINS - 1))

    orb_copy = pltpu.make_async_copy(orb_hbm, raw.at[pl.ds(0, 2800), :], load_sem.at[0])
    pot_copy = pltpu.make_async_copy(pot_hbm, pot, load_sem.at[1])
    bg_copy = pltpu.make_async_copy(bg_hbm, bg, load_sem.at[2])
    table_copies = [
        pltpu.make_async_copy(src, dst, table_sem.at[i])
        for i, (src, dst) in enumerate(
            ((qz_hbm, qz), (fy_hbm, fy), (iy_hbm, iy), (xt_hbm, xt), (xb_hbm, xb))
        )
    ]
    for copy in [orb_copy, pot_copy, bg_copy] + table_copies:
        copy.start()

    own_start = starts[d]
    thickness = starts[d + 1] - own_start
    top_row = jnp.clip(thickness - 1, 0, LAYERS - 1)
    lane = lax.broadcasted_iota(i32, (8, 128), 1)
    sub = lax.broadcasted_iota(i32, (8, 128), 0)
    radius = float((SIDE - 2) ** 2)
    x_off = (2 * (own_start + sub) - (SIDE - 1)).astype(f32)
    x_square = jnp.where(sub < thickness, x_off * x_off, 1.0e9)
    yz_parts = []
    for j in range(5):
        flat = lane + 128 * j
        y_low = (
            (flat >= SIDE).astype(i32)
            + (flat >= 2 * SIDE).astype(i32)
            + (flat >= 3 * SIDE).astype(i32)
        )
        z_off = (2 * (flat - SIDE * y_low) - (SIDE - 1)).astype(f32)
        yz_parts.append(((2 * y_low - (SIDE - 1)).astype(f32), x_square + z_off * z_off))
    is_spare = sub == 7
    is_above = sub == top_row + 1
    first_lane = lane == 0
    last_lane = lane == 127
    low_lanes = lane < 32
    high_lanes = lane >= 96

    def inside(g, j):
        y_base, xz_square = yz_parts[j]
        y_off = y_base + (8 * g).astype(f32)
        return y_off * y_off + xz_square <= radius

    def lanes_of(g, j):
        return pl.ds(pl.multiple_of(g * LANES + 128 * j, 128), 128)

    def rows_of(g):
        return pl.ds(pl.multiple_of(g * 8, 8), 8)

    def rows7_of(g):
        return pl.ds(pl.multiple_of(g * 8, 8), 7)

    def edge_sends(k, ch):
        to_low = pltpu.make_async_remote_copy(
            send_lo.at[k, ch], halo_hi.at[k, ch], send_lo_sem.at[k, ch], recv_hi_sem.at[k, ch],
            device_id=low_dev, device_id_type=MESH,
        )
        to_high = pltpu.make_async_remote_copy(
            send_hi.at[k, ch], halo_lo.at[k, ch], send_hi_sem.at[k, ch], recv_lo_sem.at[k, ch],
            device_id=high_dev, device_id_type=MESH,
        )
        return to_low, to_high

    def start_edges(k, ch):
        to_low, to_high = edge_sends(k, ch)

        @pl.when(has_low)
        def _():
            to_low.start()

        @pl.when(has_high)
        def _():
            to_high.start()

    def await_edges(k, ch):
        to_low, to_high = edge_sends(k, ch)

        @pl.when(has_low)
        def _():
            to_high.wait_recv()

        @pl.when(has_high)
        def _():
            to_low.wait_recv()

    zero = jnp.zeros((8, 128), f32)
    for cur in (cur_a, cur_b):
        for c in range(2):
            for j in range(5):
                cur[c, j, 0:8, :] = zero
                cur[c, j, 8 * GROUPS + 8 : 8 * GROUPS + 16, :] = zero

    def pick_edges(cur, k, ch):
        base = (ch * CHUNK_GROUPS + 1) * 8
        for c in range(2):
            for j in range(5):
                view = cur.at[c, j]
                send_lo[k, ch, c, j] = view[pl.ds(base, CHUNK_GROUPS, stride=8), :]
                send_hi[k, ch, c, j] = view[pl.ds(base + top_row, CHUNK_GROUPS, stride=8), :]

    @pl.when(jnp.logical_not(has_low))
    def _():
        halo_lo[...] = jnp.zeros(halo_lo.shape, f32)

    @pl.when(jnp.logical_not(has_high))
    def _():
        halo_hi[...] = jnp.zeros(halo_hi.shape, f32)

    orb_copy.wait()
    pot_copy.wait()

    def first_chunk(ch, carry):
        def first(gi, inner):
            for step_g in range(2):
                g = ch * CHUNK_GROUPS + gi * 2 + step_g
                for j in range(5):
                    keep = inside(g, j)
                    mask = jnp.where(keep, 1.0, 0.0)
                    half[j, rows_of(g), :] = 0.5 * mask
                    diag[j, rows_of(g), :] = zero
                    diag[j, rows7_of(g), :] = (3.0 + pot[:, lanes_of(g, j)]) * mask[0:7, :]
                    for c in range(2):
                        value = raw[pl.ds(c * 1400 + 5 * g + j, 8, stride=200), :]
                        value = jnp.where(keep, value, 0.0)
                        cur_a[c, j, rows_of(g + 1), :] = value
                        psi[c, j, rows_of(g), :] = value
            return inner

        lax.fori_loop(0, CHUNK_GROUPS // 2, first, 0)
        pick_edges(cur_a, 0, ch)
        return carry

    lax.fori_loop(0, CHUNKS, first_chunk, 0)
    pl.semaphore_wait(
        barrier, 13 + jnp.where(cross_low, 1, 0) + jnp.where(cross_high, 1, 0)
    )


    def send_first(ch, carry):
        start_edges(0, ch)
        return carry

    lax.fori_loop(0, CHUNKS, send_first, 0)

    for step in range(1, 4):
        pl.semaphore_signal(ready_a, inc=1, device_id=dev((s + step) & 3, d), device_id_type=MESH)

    span = 4

    def taylor(k):
        factor = time_step / k
        src, dst = (cur_a, cur_b) if k % 2 else (cur_b, cur_a)
        count = 5 * span

        def chunk(ch, carry):
            await_edges(k - 1, ch)

            def block(bi, inner):
                g0 = ch * CHUNK_GROUPS + bi * span

                def tile(c, v):
                    return src[c, v % 5, rows_of(g0 + 1 + v // 5), :]

                def turned(own, amount, cache):
                    def at(v):
                        if v not in cache:
                            cache[v] = pltpu.roll(own(v), amount, 1)
                        return cache[v]

                    return at

                for c in range(2):
                    tiles = {}

                    def own(v, c=c, tiles=tiles):
                        if v not in tiles:
                            tiles[v] = tile(c, v)
                        return tiles[v]

                    right1, left1, right32, left32 = (
                        turned(own, amount, {}) for amount in (1, 127, 32, 96)
                    )
                    to = 1 - c
                    scale = -factor if to else factor
                    for v in range(count):
                        j, gi = v % 5, bi * span + v // 5
                        g = g0 + v // 5
                        rows = rows_of(g)
                        near = jnp.where(first_lane, right1(v - 1), right1(v)) + jnp.where(
                            last_lane, left1(v + 1), left1(v)
                        )
                        far = jnp.where(low_lanes, right32(v - 2), right32(v - 1)) + jnp.where(
                            high_lanes, left32(v + 2), left32(v + 1)
                        )
                        low = jnp.broadcast_to(
                            halo_lo[k - 1, ch, c, j, pl.ds(gi, 1), :], (8, 128)
                        )
                        high = jnp.broadcast_to(
                            halo_hi[k - 1, ch, c, j, pl.ds(gi, 1), :], (8, 128)
                        )
                        stacked = pltpu.roll(
                            jnp.where(is_spare, low, own(v)), 1, 0
                        ) + pltpu.roll(jnp.where(is_above, high, own(v)), 7, 0)
                        fresh = scale * (
                            diag[j, rows, :] * own(v)
                            - half[j, rows, :] * ((near + far) + stacked)
                        )
                        value = psi[to, j, rows, :] + fresh
                        if k < TERMS:
                            dst[to, j, rows_of(g + 1), :] = fresh
                            psi[to, j, rows, :] = value
                        else:
                            raw[pl.ds(to * 1400 + 5 * g + j, 7, stride=200), :] = value[0:7, :]
                            cols = slice(128 * j, 128 * j + 128)
                            square = occ[0] * (value * value)
                            if c:
                                square = rho_own[g, :, cols] + square
                            rho_own[g, :, cols] = square
                return inner

            lax.fori_loop(0, CHUNK_GROUPS // span, block, 0)
            if k < TERMS:
                pick_edges(dst, k, ch)
                start_edges(k, ch)
                return carry
            share_rho(ch).start()
            return chip_sum(ch - 1, ch > 0, carry)

        if k < TERMS:
            return lax.fori_loop(0, CHUNKS, chunk, 0)
        return chip_sum(CHUNKS - 1, None, lax.fori_loop(0, CHUNKS, chunk, zero))

    def chip_sum(ch, live, acc):
        if live is None:
            share_rho(ch).wait_recv()
        else:

            @pl.when(live)
            def _():
                share_rho(ch).wait_recv()

        def group(gi, inner):
            g = ch * CHUNK_GROUPS + gi
            for j in range(5):
                cols = slice(128 * j, 128 * j + 128)
                value = rho_own[g, :, cols] + rho_rx[g, :, cols]
                rho_chip[g, :, cols] = value
                rho_cols[j, rows_of(g), :] = value
                inner = inner + value
            return inner

        count = CHUNK_GROUPS if live is None else jnp.where(live, CHUNK_GROUPS, 0)
        return lax.fori_loop(0, count, group, acc)

    def share_rho(ch):
        rows = pl.ds(ch * CHUNK_GROUPS, CHUNK_GROUPS)
        return pltpu.make_async_remote_copy(
            rho_own.at[rows], rho_rx.at[rows], part_send.at[ch], part_recv.at[ch],
            device_id=partner, device_id_type=MESH,
        )

    def forward_z(src):
        parts = [split(src[j]) for j in range(5)]
        for r in range(4):
            high, low = (
                jnp.concatenate([parts[r][i], parts[r + 1][i]], axis=1) for i in range(2)
            )
            out = dot(jnp.concatenate([high, high, low], axis=1), fz[r])
            za[r * 320 : (r + 1) * 320, :] = out[:, 0:128]
            zb[r * 320 : (r + 1) * 320, :] = out[:, 128:256]

    other = 1 - core

    def forward_y(dst, slots):
        table = fy[other]
        for slot in slots:
            rows = pl.ds(slot, SIDE, stride=8)
            right = jnp.concatenate([za[rows, :], zb[rows, :]], axis=1)
            out = dot(table, stack_right(right))
            dst[pl.ds(slot, 96, stride=8), :] = out[:, 0:128]
            tail = out[:, 128:256]
            packed = tail[0:24, :]
            for j in range(1, 4):
                packed = packed + pltpu.roll(tail[24 * j : 24 * j + 24, :], 32 * j, 1)
            dst[pl.ds(96 * 8 + slot, 24, stride=8), :] = packed

    def put_total(dst, partial):
        total = jnp.broadcast_to(jnp.sum(partial, axis=0, keepdims=True), (120, 128))
        dst[pl.ds(7, 120, stride=8), :] = total

    pair_of = (chip * 25 + 31) >> 5
    is_owner = jnp.logical_and(lax.div(pair_of * 32, 25) == chip, pair_of < PAIRS)

    def build_x_tables():
        @pl.when(is_owner)
        def _():
            lane256 = lax.broadcasted_iota(i32, (SIDE, 256), 1)
            row160 = lax.broadcasted_iota(i32, (SIDE, 256), 0)
            lane_row = lax.broadcasted_iota(i32, (8, 256), 1)
            slot_row = lane_row % 8
            dom_row = lane_row // 8
            where_x = jnp.full((8, 256), -1, i32)
            pieces = []
            sub256 = lax.broadcasted_iota(i32, (8, 256), 0)
            for k in range(DOMAINS):
                first_x = starts[k]
                count = starts[k + 1] - first_x
                where_x = jnp.where(
                    jnp.logical_and(dom_row == k, slot_row < count), first_x + slot_row, where_x
                )
                hit = jnp.logical_and(lane_row == first_x + sub256, sub256 < count)
                pieces.append(jnp.where(hit, 1.0, 0.0))
            select_back = jnp.concatenate(pieces, axis=0).astype(bf16)
            wide_x = jnp.broadcast_to(where_x[0:1, :], (256, 256))
            row256 = lax.broadcasted_iota(i32, (256, 256), 0)
            select = jnp.where(wide_x == row256, 1.0, 0.0).astype(bf16)
            x_high, x_low = (dot(xt[i], select).astype(bf16) for i in range(2))
            x_fwd[...] = jnp.concatenate([x_high, x_high, x_low], axis=1)
            for i in range(2):
                x_inv[i] = dot(select_back, xb[i]).astype(bf16)
            o = 2 * pair_of + core
            unit = 2 * o + lane256 // 128
            low_lane = lane256 % 128
            is_tail = unit >= SIDE
            ky = jnp.where(is_tail, 40 * (low_lane // 32) + unit - SIDE, unit)
            kz = jnp.where(is_tail, 128 + low_lane % 32, low_lane)

            def wave(index):
                folded = jnp.where(2 * index <= SIDE, index, index - SIDE // 2)
                number = folded.astype(f32) * (two_pi / SIDE)
                return number * number

            squared = wave(row160) + wave(ky) + wave(kz)
            coulomb[...] = jnp.where(squared > 0, four_pi / jnp.where(squared > 0, squared, 1.0), 0.0)


    bg_copy.wait()

    def ion_group(g, acc):
        for j in range(5):
            weight = 2.0 * half[j, rows_of(g), :]
            ion[j, rows_of(g), :] = zero
            ion[j, rows7_of(g), :] = bg[:, lanes_of(g, j)] * weight[0:7, :]
            acc = acc + ion[j, rows_of(g), :]
        return acc

    ion_total = lax.fori_loop(0, GROUPS, ion_group, zero)
    for copy in table_copies:
        copy.wait()
    fz[...] = jnp.zeros(fz.shape, bf16)
    for i, which in enumerate((0, 1, 0)):
        for r in range(4):
            fz[r, 256 * i + 32 * r : 256 * i + 32 * r + SIDE, :] = qz[which]
    forward_z(ion)

    forward_y(e_ion, range(0, 4))
    taylor(1)
    forward_y(e_ion, range(4, 7))
    put_total(e_ion, ion_total)

    pl.semaphore_wait(ready_a, 3)
    for step in range(1, 4):
        pl.semaphore_signal(
            ready_b, inc=1, device_id=dev(s, (d + 8 * step) & (DOMAINS - 1)), device_id_type=MESH
        )

    taylor(2)
    build_x_tables()
    taylor(3)
    pl.semaphore_wait(ready_b, 3)

    def div(value, by):
        return lax.div(value, jnp.int32(by))

    def owner_dev(p):
        place_of = p + div(p * 7, 25)
        return dev((place_of & 1) * 2 + other, place_of >> 1)

    def sent_rows(p):
        tens = div(p, 10)
        return pl.ds(pl.multiple_of((4 * tens + 2 * p) * 8, 16), 16)

    def column_rows(p, half_of):
        return pl.ds(pl.multiple_of((2 * p + half_of) * 16, 16), 16)

    def wrap(value, count):
        return jnp.where(value >= count, value - count, value)

    ion_first = lax.rem(d, jnp.int32(25))
    rho_first = (chip * 25) >> 5

    def send_ion(j):
        p = 2 * wrap(j + ion_first, 25) + ylo
        return pltpu.make_async_remote_copy(
            e_ion.at[sent_rows(p), :],
            recv_ion.at[pl.ds(pl.multiple_of(d * 16, 16), 16), :],
            ion_send, ion_recv, device_id=owner_dev(p), device_id_type=MESH,
        )

    def send_rho(j):
        p = wrap(j + rho_first, PAIRS)
        return pltpu.make_async_remote_copy(
            e_rho.at[sent_rows(p), :],
            recv_rho.at[pl.ds(pl.multiple_of((ylo * DOMAINS + d) * 16, 16), 16), :],
            fwd_send, rho_recv, device_id=owner_dev(p), device_id_type=MESH,
        )

    def start_all(make, count):
        def one(j, carry):
            make(j).start()
            return carry

        lax.fori_loop(0, count, one, 0)

    start_all(send_ion, 25)

    rho_total = taylor(4)
    psi_copy = pltpu.make_async_copy(raw.at[pl.ds(0, 2800), :], psi_out, out_sem.at[0])
    psi_copy.start()

    forward_z(rho_cols)
    forward_y(e_rho, range(7))
    put_total(e_rho, rho_total)
    start_all(send_rho, PAIRS)

    def share_sum(part):
        return pltpu.make_async_remote_copy(
            rho_chip.at[pl.ds(core * 20 + 10 * part, 10)], rho_y.at[pl.ds(10 * part, 10)],
            y_send.at[part], y_recv.at[part], device_id=across, device_id_type=MESH,
        )

    share_sum(0).start()

    def await_bytes(ref, sem):
        pltpu.make_async_copy(ref, ref, sem).wait()

    def send_back(j):
        q = (j + chip) & (CHIPS - 1)
        return pltpu.make_async_remote_copy(
            result.at[pl.ds(pl.multiple_of((q >> 1) * 16, 16), 16), :],
            spec.at[pl.ds(pl.multiple_of((2 * pair_of + core) * 16, 16), 16), :],
            back_send, back_recv,
            device_id=dev((q & 1) * 2 + other, q >> 1), device_id_type=MESH,
        )

    @pl.when(is_owner)
    def _():
        await_bytes(recv_ion, ion_recv)
        await_bytes(recv_rho, rho_recv)
        ions = recv_ion[...].reshape(DOMAINS, 2, 8, 128)
        dens = recv_rho[...].reshape(2, DOMAINS, 2, 8, 128)
        dens = dens[0] + dens[1]
        sub8 = lax.broadcasted_iota(i32, (8, 128), 0)

        def total_of(array):
            rows = jnp.sum(array[:, 0], axis=0)
            return jnp.sum(jnp.where(sub8 == 7, rows, 0.0), axis=(0, 1), keepdims=True)

        scale = total_of(dens) / total_of(ions)
        charge = dens - scale.reshape(1, 1, 1, 1) * ions
        right = jnp.concatenate(
            [charge[:, 0].reshape(256, 128), charge[:, 1].reshape(256, 128)], axis=1
        )
        waves = dot(x_fwd[...], stack_right(right)) * coulomb[...]
        w_high, w_low = split(waves)
        back = dot(x_inv[0], w_high) + (dot(x_inv[0], w_low) + dot(x_inv[1], w_high))
        result[...] = jnp.stack(
            [back[:, 0:128].reshape(DOMAINS, 8, 128), back[:, 128:256].reshape(DOMAINS, 8, 128)],
            axis=1,
        ).reshape(DOMAINS * 16, 128)
        start_all(send_back, CHIPS)

    share_sum(1).start()

    def root(i, carry):
        value = (3.0 / math.pi) * (rho_chip[core * 20 + i] + rho_y[i])
        positive = value > 1.0e-37
        safe = jnp.where(positive, value, 1.0)
        guess = jnp.exp(jnp.log(safe) * (1.0 / 3.0))
        guess = (2.0 * guess + safe / (guess * guess)) * (1.0 / 3.0)
        xc[core * 20 + i] = jnp.where(positive, guess, 0.0)
        return carry

    def share_root(part):
        rows = pl.ds(core * 20 + 10 * part, 10)
        return pltpu.make_async_remote_copy(
            xc.at[rows], xc.at[rows], xc_send.at[part], xc_recv.at[part],
            device_id=partner, device_id_type=MESH,
        )

    share_sum(0).wait_recv()
    lax.fori_loop(0, 10, root, 0)
    share_root(0).start()

    await_bytes(spec.at[pl.ds(0, 800), :], back_recv)

    halves_of = spec.reshape(PAIRS, 32, 128).at[:, pl.ds(pl.multiple_of(other * 16, 16), 16), :]
    swap = pltpu.make_async_remote_copy(
        halves_of, halves_of, mid_send, mid_recv, device_id=partner, device_id_type=MESH
    )
    swap.start()
    await_bytes(spec.at[pl.ds(0, 800), :], mid_recv)

    for slot in range(7):
        rows = pl.ds(slot, SIDE, stride=8)
        main = spec[rows, :]
        tail = spec[pl.ds(SIDE * 8 + slot, 40, stride=8), :]
        parts = [tail] + [pltpu.roll(tail, 128 - 32 * j, 1) for j in range(1, 4)]
        right = jnp.concatenate([main, jnp.concatenate(parts, axis=0)], axis=1)
        out = dot(iy[...], stack_right(right))
        za[rows, :] = out[:, 0:128]
        zb[rows, :] = out[:, 128:256]
    share_sum(1).wait_recv()
    lax.fori_loop(10, 20, root, 0)
    share_root(1).start()
    carried = None
    for r in range(4):
        left = jnp.concatenate(
            [za[r * 320 : (r + 1) * 320, :], zb[r * 320 : (r + 1) * 320, :]], axis=1
        )
        high, low = split(left)
        out = dot_t(high, fz[r, 0:256, :] ) + dot_t(high, fz[r, 256:512, :])
        out = out + dot_t(low, fz[r, 0:256, :])
        piece = out[:, 0:128]
        if carried is not None:
            piece = piece + carried
        hsc[r] = piece
        carried = out[:, 128:256]
    hsc[4] = carried

    share_root(0).wait_recv()
    share_root(1).wait_recv()

    def finish(g, carry):
        for j in range(5):
            value = hsc[j, rows_of(g), :] - xc[g, :, 128 * j : 128 * j + 128]
            value = jnp.where(half[j, rows_of(g), :] > 0.0, value, 0.0)
            field[:, lanes_of(g, j)] = value[0:7, :]
        return carry

    lax.fori_loop(0, GROUPS, finish, 0)
    field_copy = pltpu.make_async_copy(field, field_out, out_sem.at[1])
    field_copy.start()

    for k in range(TERMS):
        def drain(ch, carry, k=k):
            to_low, to_high = edge_sends(k, ch)

            @pl.when(has_low)
            def _():
                to_low.wait_send()

            @pl.when(has_high)
            def _():
                to_high.wait_send()

            return carry

        lax.fori_loop(0, CHUNKS, drain, 0)

    def drain_rho(ch, carry):
        share_rho(ch).wait_send()
        return carry

    lax.fori_loop(0, CHUNKS, drain_rho, 0)
    for part in range(2):
        share_sum(part).wait_send()
        share_root(part).wait_send()
    await_bytes(e_ion.at[pl.ds(0, 400), :], ion_send)
    await_bytes(e_rho.at[pl.ds(0, 800), :], fwd_send)
    await_bytes(spec.at[pl.ds(0, 800), :], mid_send)

    @pl.when(is_owner)
    def _():
        await_bytes(recv_rho, back_send)

    psi_copy.wait()
    field_copy.wait()


def hand_over(psi_in, field_in, psi_out, field_out, psi_buf, field_buf, sems):
    moves = []
    for i in range(4):
        rows = pl.ds(704 * i, 704 if i < 3 else 688)
        moves.append((psi_in.at[rows, :], psi_buf.at[rows, :], psi_out.at[rows, :]))
    for i in range(2):
        lanes = pl.ds(12800 * i, 12800)
        moves.append((field_in.at[:, lanes], field_buf.at[:, lanes], field_out.at[:, lanes]))
    reads = [pltpu.make_async_copy(a, b, sems.at[0, i]) for i, (a, b, _) in enumerate(moves)]
    writes = [pltpu.make_async_copy(b, c, sems.at[1, i]) for i, (_, b, c) in enumerate(moves)]
    for read in reads:
        read.start()
    for read, write in zip(reads, writes):
        read.wait()
        write.start()
    for write in writes:
        write.wait()


def step(orbitals, occupation, potential, background, layer_start):
    tabs = [jnp.asarray(t) for t in tables()]
    vmem = lambda *shape: pltpu.VMEM(shape, f32)
    dma = pltpu.SemaphoreType.DMA
    anyspace = pl.BlockSpec(memory_space=pl.ANY)
    smem = pl.BlockSpec(memory_space=pltpu.SMEM)
    edge = (TERMS, CHUNKS, 2, 5, CHUNK_GROUPS, 128)
    cube = (GROUPS, 8, LANES)
    columns = (1600, 128)
    tile5 = (5, 8 * GROUPS, 128)
    padded = (2, 5, 8 * GROUPS + 16, 128)
    scratch = [
        vmem(3000, 128), vmem(LAYERS, PLANE), vmem(LAYERS, PLANE),
        *[pltpu.VMEM(t.shape, bf16) for t in tabs],
        pltpu.VMEM((4, 768, 256), bf16),
        vmem(*padded), vmem(*padded), vmem(2, *tile5), vmem(*tile5), vmem(*tile5), vmem(*tile5),
        vmem(*edge), vmem(*edge), vmem(*edge), vmem(*edge),
        vmem(*cube), vmem(*cube), vmem(*cube), vmem(*tile5), vmem(20, 8, LANES), vmem(*cube),
        vmem(1280, 128), vmem(1280, 128), vmem(960, 128), vmem(960, 128),
        vmem(1024, 128), vmem(512, 128), vmem(512, 128), vmem(*columns),
        vmem(*tile5), vmem(LAYERS, PLANE),
        pltpu.VMEM((SIDE, 768), bf16), pltpu.VMEM((2, 256, SIDE), bf16), vmem(SIDE, 256),
        dma((3,)), dma((5,)), dma((2,)),
        dma((TERMS, CHUNKS)), dma((TERMS, CHUNKS)), dma((TERMS, CHUNKS)), dma((TERMS, CHUNKS)),
        dma((CHUNKS,)), dma((CHUNKS,)),
        *[dma((2,)) for _ in range(4)],
        *[dma(()) for _ in range(8)],
        pltpu.SemaphoreType.REGULAR, pltpu.SemaphoreType.REGULAR,
    ]
    psi, field = pl.pallas_call(
        kernel,
        out_shape=(
            jax.ShapeDtypeStruct((2800, 128), f32),
            jax.ShapeDtypeStruct((LAYERS, PLANE), f32),
        ),
        in_specs=[smem, smem] + [anyspace] * 8,
        out_specs=(anyspace, anyspace),
        scratch_shapes=scratch,
        compiler_params=pltpu.CompilerParams(
            collective_id=0, has_side_effects=True, vmem_limit_bytes=60 * 1024 * 1024
        ),
    )(
        layer_start, occupation, orbitals.reshape(2800, 128), potential, background, *tabs
    )
    psi, field = pl.pallas_call(
        hand_over,
        out_shape=(
            jax.ShapeDtypeStruct((2800, 128), f32),
            jax.ShapeDtypeStruct((LAYERS, PLANE), f32),
        ),
        in_specs=[anyspace, anyspace],
        out_specs=(anyspace, anyspace),
        scratch_shapes=[vmem(2800, 128), vmem(LAYERS, PLANE), dma((2, 6))],
        compiler_params=pltpu.CompilerParams(vmem_limit_bytes=60 * 1024 * 1024),
    )(psi, field)
    return psi.reshape(2, 1, LAYERS, PLANE), field


def solution(mesh):
    return jax.shard_map(
        step,
        mesh=mesh,
        in_specs=(
            P(None, "state", "domain", None),
            P("state"),
            P("domain", None),
            P("domain", None),
            P(),
        ),
        out_specs=(P(None, "state", "domain", None), P("domain", None)),
        check_vma=False,
    )
```

```python
import functools
import math

import jax
import jax.numpy as jnp
import numpy as np
from jax import lax
from jax.experimental import pallas as pl
from jax.experimental.pallas import tpu as pltpu
from jax.sharding import PartitionSpec as P

SIDE = 160
SLAB = 5
TERMS = 4
LAYERS = 7
PLANE = SIDE * SIDE
GROUPS = 40
LANES = 640
CHUNKS = 10
CHUNK_GROUPS = 4
OWNERS = 100
PAIRS = 50
DOMAINS = 32
STATES = 4
CHIPS = 64

time_step = 0.3
four_pi = 4.0 * math.pi
two_pi = 2.0 * math.pi
MESH = pl.DeviceIdType.MESH
f32 = jnp.float32
i32 = jnp.int32
bf16 = jnp.bfloat16


def halves(table):
    table = np.asarray(table, np.float32)
    high = table.astype(bf16)
    low = (table - high.astype(np.float32)).astype(bf16)
    return np.stack([high, low])


def real_basis():
    n = SIDE
    j = np.arange(n)
    rows = []
    for i in range(n):
        if i == 0:
            rows.append(np.full(n, math.sqrt(1.0 / n)))
        elif i < n // 2:
            rows.append(math.sqrt(2.0 / n) * np.cos(2 * np.pi * ((i * j) % n) / n))
        elif i == n // 2:
            rows.append(math.sqrt(1.0 / n) * np.where(j % 2 == 0, 1.0, -1.0))
        else:
            m = i - n // 2
            rows.append(math.sqrt(2.0 / n) * np.sin(2 * np.pi * ((m * j) % n) / n))
    return np.stack(rows)


def tables():
    q = real_basis()
    side_table = np.zeros((SIDE, 256))
    side_table[:, :SIDE] = q.T
    order = np.array([4 * g + r for r in range(4) for g in range(GROUPS)])
    forward_y = q[:, order]
    x_table = np.zeros((SIDE, 256))
    x_table[:, :SIDE] = q
    x_back = np.zeros((256, SIDE))
    x_back[:SIDE, :] = q.T
    half_y = np.zeros((2, 96, SIDE))
    for which in range(2):
        for j in range(4):
            for q in range(20):
                half_y[which, 24 * j + q] = forward_y[40 * j + 4 * (q // 2) + 2 * which + q % 2]
    high, low = halves(half_y)
    left_y = np.concatenate([high, high, low], axis=2)
    high, low = halves(forward_y.T)
    left_back = np.concatenate([high, high, low], axis=1)
    return [halves(side_table), left_y, left_back, halves(x_table), halves(x_back)]


def split(value):
    high = value.astype(bf16)
    low = (value - high.astype(f32)).astype(bf16)
    return high, low


def dot(a, b):
    return jnp.dot(a, b, preferred_element_type=f32)


def dot_t(a, b):
    dims = (((1,), (1,)), ((), ()))
    return lax.dot_general(a, b, dims, preferred_element_type=f32)


def stack_left(value, axis=1):
    high, low = split(value)
    return jnp.concatenate([high, high, low], axis=axis)


def stack_right(value, axis=0):
    high, low = split(value)
    return jnp.concatenate([high, low, high], axis=axis)


def kernel(
    starts, occ, orb_hbm, pot_hbm, bg_hbm, qz_hbm, fy_hbm, iy_hbm, xt_hbm, xb_hbm,
    psi_out, field_out,
    raw, pot, bg, qz, fy, iy, xt, xb, fz,
    cur_a, cur_b, psi, diag, half, ion,
    send_lo, send_hi, halo_lo, halo_hi,
    rho_own, rho_rx, rho_chip, rho_cols, rho_y, xc,
    za, zb, e_rho, e_ion, recv_rho, recv_ion, result, spec, hsc, field,
    x_fwd, x_inv, coulomb,
    load_sem, table_sem, out_sem,
    send_lo_sem, send_hi_sem, recv_lo_sem, recv_hi_sem,
    part_send, part_recv, y_send, y_recv, xc_send, xc_recv,
    fwd_send, rho_recv, ion_send, ion_recv, back_send, back_recv, mid_send, mid_recv,
    ready_a, ready_b,
):
    s = lax.axis_index("state")
    d = lax.axis_index("domain")
    core = s & 1
    ylo = s >> 1
    chip = d * 2 + ylo

    def dev(state, domain):
        return {"state": state, "domain": domain}

    partner = dev(ylo * 2 + 1 - core, d)
    across = dev((1 - ylo) * 2 + core, d)
    has_low = d > 0
    has_high = d < DOMAINS - 1
    low_dev = dev(s, jnp.maximum(d - 1, 0))
    high_dev = dev(s, jnp.minimum(d + 1, DOMAINS - 1))
    octet = d >> 3
    place = d & 7

    barrier = pltpu.get_barrier_semaphore()

    def greet(state, domain):
        pl.semaphore_signal(barrier, inc=1, device_id=dev(state, domain), device_id_type=MESH)

    for step in range(1, 8):
        greet(s, octet * 8 + ((place + step) & 7))
    for step in range(1, 4):
        greet((s + step) & 3, d)
        greet(s, (d + 8 * step) & (DOMAINS - 1))
    cross_low = jnp.logical_and(place == 0, has_low)
    cross_high = jnp.logical_and(place == 7, has_high)

    @pl.when(cross_low)
    def _():
        greet(s, jnp.maximum(d - 1, 0))

    @pl.when(cross_high)
    def _():
        greet(s, jnp.minimum(d + 1, DOMAINS - 1))

    orb_copy = pltpu.make_async_copy(orb_hbm, raw.at[pl.ds(0, 2800), :], load_sem.at[0])
    pot_copy = pltpu.make_async_copy(pot_hbm, pot, load_sem.at[1])
    bg_copy = pltpu.make_async_copy(bg_hbm, bg, load_sem.at[2])
    table_copies = [
        pltpu.make_async_copy(src, dst, table_sem.at[i])
        for i, (src, dst) in enumerate(
            ((qz_hbm, qz), (fy_hbm, fy), (iy_hbm, iy), (xt_hbm, xt), (xb_hbm, xb))
        )
    ]
    for copy in [orb_copy, pot_copy, bg_copy] + table_copies:
        copy.start()

    own_start = starts[d]
    thickness = starts[d + 1] - own_start
    top_row = jnp.clip(thickness - 1, 0, LAYERS - 1)
    lane = lax.broadcasted_iota(i32, (8, 128), 1)
    sub = lax.broadcasted_iota(i32, (8, 128), 0)
    radius = float((SIDE - 2) ** 2)
    x_off = (2 * (own_start + sub) - (SIDE - 1)).astype(f32)
    x_square = jnp.where(sub < thickness, x_off * x_off, 1.0e9)
    yz_parts = []
    for j in range(5):
        flat = lane + 128 * j
        y_low = (
            (flat >= SIDE).astype(i32)
            + (flat >= 2 * SIDE).astype(i32)
            + (flat >= 3 * SIDE).astype(i32)
        )
        z_off = (2 * (flat - SIDE * y_low) - (SIDE - 1)).astype(f32)
        yz_parts.append(((2 * y_low - (SIDE - 1)).astype(f32), x_square + z_off * z_off))
    is_spare = sub == 7
    is_above = sub == top_row + 1
    first_lane = lane == 0
    last_lane = lane == 127
    low_lanes = lane < 32
    high_lanes = lane >= 96

    def inside(g, j):
        y_base, xz_square = yz_parts[j]
        y_off = y_base + (8 * g).astype(f32)
        return y_off * y_off + xz_square <= radius

    def lanes_of(g, j):
        return pl.ds(pl.multiple_of(g * LANES + 128 * j, 128), 128)

    def rows_of(g):
        return pl.ds(pl.multiple_of(g * 8, 8), 8)

    def rows7_of(g):
        return pl.ds(pl.multiple_of(g * 8, 8), 7)

    def edge_sends(k, ch):
        to_low = pltpu.make_async_remote_copy(
            send_lo.at[k, ch], halo_hi.at[k, ch], send_lo_sem.at[k, ch], recv_hi_sem.at[k, ch],
            device_id=low_dev, device_id_type=MESH,
        )
        to_high = pltpu.make_async_remote_copy(
            send_hi.at[k, ch], halo_lo.at[k, ch], send_hi_sem.at[k, ch], recv_lo_sem.at[k, ch],
            device_id=high_dev, device_id_type=MESH,
        )
        return to_low, to_high

    def start_edges(k, ch):
        to_low, to_high = edge_sends(k, ch)

        @pl.when(has_low)
        def _():
            to_low.start()

        @pl.when(has_high)
        def _():
            to_high.start()

    def await_edges(k, ch):
        to_low, to_high = edge_sends(k, ch)

        @pl.when(has_low)
        def _():
            to_high.wait_recv()

        @pl.when(has_high)
        def _():
            to_low.wait_recv()

    zero = jnp.zeros((8, 128), f32)
    for cur in (cur_a, cur_b):
        for c in range(2):
            for j in range(5):
                cur[c, j, 0:8, :] = zero
                cur[c, j, 8 * GROUPS + 8 : 8 * GROUPS + 16, :] = zero

    def pick_edges(cur, k, ch):
        base = (ch * CHUNK_GROUPS + 1) * 8
        for c in range(2):
            for j in range(5):
                view = cur.at[c, j]
                send_lo[k, ch, c, j] = view[pl.ds(base, CHUNK_GROUPS, stride=8), :]
                send_hi[k, ch, c, j] = view[pl.ds(base + top_row, CHUNK_GROUPS, stride=8), :]

    @pl.when(jnp.logical_not(has_low))
    def _():
        halo_lo[...] = jnp.zeros(halo_lo.shape, f32)

    @pl.when(jnp.logical_not(has_high))
    def _():
        halo_hi[...] = jnp.zeros(halo_hi.shape, f32)

    orb_copy.wait()
    pot_copy.wait()

    def first_chunk(ch, carry):
        def first(gi, inner):
            for step_g in range(2):
                g = ch * CHUNK_GROUPS + gi * 2 + step_g
                for j in range(5):
                    keep = inside(g, j)
                    mask = jnp.where(keep, 1.0, 0.0)
                    half[j, rows_of(g), :] = 0.5 * mask
                    diag[j, rows_of(g), :] = zero
                    diag[j, rows7_of(g), :] = (3.0 + pot[:, lanes_of(g, j)]) * mask[0:7, :]
                    for c in range(2):
                        value = raw[pl.ds(c * 1400 + 5 * g + j, 8, stride=200), :]
                        value = jnp.where(keep, value, 0.0)
                        cur_a[c, j, rows_of(g + 1), :] = value
                        psi[c, j, rows_of(g), :] = value
            return inner

        lax.fori_loop(0, CHUNK_GROUPS // 2, first, 0)
        pick_edges(cur_a, 0, ch)
        return carry

    lax.fori_loop(0, CHUNKS, first_chunk, 0)
    pl.semaphore_wait(
        barrier, 13 + jnp.where(cross_low, 1, 0) + jnp.where(cross_high, 1, 0)
    )


    def send_first(ch, carry):
        start_edges(0, ch)
        return carry

    lax.fori_loop(0, CHUNKS, send_first, 0)

    for step in range(1, 4):
        pl.semaphore_signal(ready_a, inc=1, device_id=dev((s + step) & 3, d), device_id_type=MESH)

    span = 4

    def taylor(k):
        factor = time_step / k
        src, dst = (cur_a, cur_b) if k % 2 else (cur_b, cur_a)
        count = 5 * span

        def chunk(ch, carry):
            await_edges(k - 1, ch)

            def block(bi, inner):
                g0 = ch * CHUNK_GROUPS + bi * span

                def tile(c, v):
                    return src[c, v % 5, rows_of(g0 + 1 + v // 5), :]

                def turned(own, amount, cache):
                    def at(v):
                        if v not in cache:
                            cache[v] = pltpu.roll(own(v), amount, 1)
                        return cache[v]

                    return at

                for c in range(2):
                    tiles = {}

                    def own(v, c=c, tiles=tiles):
                        if v not in tiles:
                            tiles[v] = tile(c, v)
                        return tiles[v]

                    right1, left1, right32, left32 = (
                        turned(own, amount, {}) for amount in (1, 127, 32, 96)
                    )
                    to = 1 - c
                    scale = -factor if to else factor
                    for v in range(count):
                        j, gi = v % 5, bi * span + v // 5
                        g = g0 + v // 5
                        rows = rows_of(g)
                        near = jnp.where(first_lane, right1(v - 1), right1(v)) + jnp.where(
                            last_lane, left1(v + 1), left1(v)
                        )
                        far = jnp.where(low_lanes, right32(v - 2), right32(v - 1)) + jnp.where(
                            high_lanes, left32(v + 2), left32(v + 1)
                        )
                        low = jnp.broadcast_to(
                            halo_lo[k - 1, ch, c, j, pl.ds(gi, 1), :], (8, 128)
                        )
                        high = jnp.broadcast_to(
                            halo_hi[k - 1, ch, c, j, pl.ds(gi, 1), :], (8, 128)
                        )
                        stacked = pltpu.roll(
                            jnp.where(is_spare, low, own(v)), 1, 0
                        ) + pltpu.roll(jnp.where(is_above, high, own(v)), 7, 0)
                        fresh = scale * (
                            diag[j, rows, :] * own(v)
                            - half[j, rows, :] * ((near + far) + stacked)
                        )
                        value = psi[to, j, rows, :] + fresh
                        if k < TERMS:
                            dst[to, j, rows_of(g + 1), :] = fresh
                            psi[to, j, rows, :] = value
                        else:
                            raw[pl.ds(to * 1400 + 5 * g + j, 7, stride=200), :] = value[0:7, :]
                            cols = slice(128 * j, 128 * j + 128)
                            square = occ[0] * (value * value)
                            if c:
                                square = rho_own[g, :, cols] + square
                            rho_own[g, :, cols] = square
                return inner

            lax.fori_loop(0, CHUNK_GROUPS // span, block, 0)
            if k < TERMS:
                pick_edges(dst, k, ch)
                start_edges(k, ch)
                return carry
            share_rho(ch).start()
            return chip_sum(ch - 1, ch > 0, carry)

        if k < TERMS:
            return lax.fori_loop(0, CHUNKS, chunk, 0)
        return chip_sum(CHUNKS - 1, None, lax.fori_loop(0, CHUNKS, chunk, zero))

    def chip_sum(ch, live, acc):
        if live is None:
            share_rho(ch).wait_recv()
        else:

            @pl.when(live)
            def _():
                share_rho(ch).wait_recv()

        def group(gi, inner):
            g = ch * CHUNK_GROUPS + gi
            for j in range(5):
                cols = slice(128 * j, 128 * j + 128)
                value = rho_own[g, :, cols] + rho_rx[g, :, cols]
                rho_chip[g, :, cols] = value
                rho_cols[j, rows_of(g), :] = value
                inner = inner + value
            return inner

        count = CHUNK_GROUPS if live is None else jnp.where(live, CHUNK_GROUPS, 0)
        return lax.fori_loop(0, count, group, acc)

    def share_rho(ch):
        rows = pl.ds(ch * CHUNK_GROUPS, CHUNK_GROUPS)
        return pltpu.make_async_remote_copy(
            rho_own.at[rows], rho_rx.at[rows], part_send.at[ch], part_recv.at[ch],
            device_id=partner, device_id_type=MESH,
        )

    def forward_z(src):
        parts = [split(src[j]) for j in range(5)]
        for r in range(4):
            high, low = (
                jnp.concatenate([parts[r][i], parts[r + 1][i]], axis=1) for i in range(2)
            )
            out = dot(jnp.concatenate([high, high, low], axis=1), fz[r])
            za[r * 320 : (r + 1) * 320, :] = out[:, 0:128]
            zb[r * 320 : (r + 1) * 320, :] = out[:, 128:256]

    other = 1 - core

    def forward_y(dst, slots):
        table = fy[other]
        for slot in slots:
            rows = pl.ds(slot, SIDE, stride=8)
            right = jnp.concatenate([za[rows, :], zb[rows, :]], axis=1)
            out = dot(table, stack_right(right))
            dst[pl.ds(slot, 96, stride=8), :] = out[:, 0:128]
            tail = out[:, 128:256]
            packed = tail[0:24, :]
            for j in range(1, 4):
                packed = packed + pltpu.roll(tail[24 * j : 24 * j + 24, :], 32 * j, 1)
            dst[pl.ds(96 * 8 + slot, 24, stride=8), :] = packed

    def put_total(dst, partial):
        total = jnp.broadcast_to(jnp.sum(partial, axis=0, keepdims=True), (120, 128))
        dst[pl.ds(7, 120, stride=8), :] = total

    pair_of = (chip * 25 + 31) >> 5
    is_owner = jnp.logical_and(lax.div(pair_of * 32, 25) == chip, pair_of < PAIRS)

    def build_x_tables():
        @pl.when(is_owner)
        def _():
            lane256 = lax.broadcasted_iota(i32, (SIDE, 256), 1)
            row160 = lax.broadcasted_iota(i32, (SIDE, 256), 0)
            lane_row = lax.broadcasted_iota(i32, (8, 256), 1)
            slot_row = lane_row % 8
            dom_row = lane_row // 8
            where_x = jnp.full((8, 256), -1, i32)
            pieces = []
            sub256 = lax.broadcasted_iota(i32, (8, 256), 0)
            for k in range(DOMAINS):
                first_x = starts[k]
                count = starts[k + 1] - first_x
                where_x = jnp.where(
                    jnp.logical_and(dom_row == k, slot_row < count), first_x + slot_row, where_x
                )
                hit = jnp.logical_and(lane_row == first_x + sub256, sub256 < count)
                pieces.append(jnp.where(hit, 1.0, 0.0))
            select_back = jnp.concatenate(pieces, axis=0).astype(bf16)
            wide_x = jnp.broadcast_to(where_x[0:1, :], (256, 256))
            row256 = lax.broadcasted_iota(i32, (256, 256), 0)
            select = jnp.where(wide_x == row256, 1.0, 0.0).astype(bf16)
            x_high, x_low = (dot(xt[i], select).astype(bf16) for i in range(2))
            x_fwd[...] = jnp.concatenate([x_high, x_high, x_low], axis=1)
            for i in range(2):
                x_inv[i] = dot(select_back, xb[i]).astype(bf16)
            o = 2 * pair_of + core
            unit = 2 * o + lane256 // 128
            low_lane = lane256 % 128
            is_tail = unit >= SIDE
            ky = jnp.where(is_tail, 40 * (low_lane // 32) + unit - SIDE, unit)
            kz = jnp.where(is_tail, 128 + low_lane % 32, low_lane)

            def wave(index):
                folded = jnp.where(2 * index <= SIDE, index, index - SIDE // 2)
                number = folded.astype(f32) * (two_pi / SIDE)
                return number * number

            squared = wave(row160) + wave(ky) + wave(kz)
            coulomb[...] = jnp.where(squared > 0, four_pi / jnp.where(squared > 0, squared, 1.0), 0.0)


    bg_copy.wait()

    def ion_group(g, acc):
        for j in range(5):
            weight = 2.0 * half[j, rows_of(g), :]
            ion[j, rows_of(g), :] = zero
            ion[j, rows7_of(g), :] = bg[:, lanes_of(g, j)] * weight[0:7, :]
            acc = acc + ion[j, rows_of(g), :]
        return acc

    ion_total = lax.fori_loop(0, GROUPS, ion_group, zero)
    for copy in table_copies:
        copy.wait()
    fz[...] = jnp.zeros(fz.shape, bf16)
    for i, which in enumerate((0, 1, 0)):
        for r in range(4):
            fz[r, 256 * i + 32 * r : 256 * i + 32 * r + SIDE, :] = qz[which]
    forward_z(ion)

    forward_y(e_ion, range(0, 4))
    taylor(1)
    forward_y(e_ion, range(4, 7))
    put_total(e_ion, ion_total)

    pl.semaphore_wait(ready_a, 3)
    for step in range(1, 4):
        pl.semaphore_signal(
            ready_b, inc=1, device_id=dev(s, (d + 8 * step) & (DOMAINS - 1)), device_id_type=MESH
        )

    taylor(2)
    build_x_tables()
    taylor(3)
    pl.semaphore_wait(ready_b, 3)

    def owner_dev(p):
        place_of = p + ((p * (7 * 5243)) >> 17)
        return dev((place_of & 1) * 2 + other, place_of >> 1)

    def sent_rows(p):
        tens = (p * 205) >> 11
        return pl.ds(pl.multiple_of((4 * tens + 2 * p) * 8, 16), 16)

    def column_rows(p, half_of):
        return pl.ds(pl.multiple_of((2 * p + half_of) * 16, 16), 16)

    def wrap(value, count):
        return jnp.where(value >= count, value - count, value)

    ion_first = lax.rem(d, jnp.int32(25))
    rho_first = (chip * 25) >> 5

    def send_ion(j):
        p = 2 * wrap(j + ion_first, 25) + ylo
        return pltpu.make_async_remote_copy(
            e_ion.at[sent_rows(p), :],
            recv_ion.at[pl.ds(pl.multiple_of(d * 16, 16), 16), :],
            ion_send, ion_recv, device_id=owner_dev(p), device_id_type=MESH,
        )

    def send_rho(j):
        p = wrap(j + rho_first, PAIRS)
        return pltpu.make_async_remote_copy(
            e_rho.at[sent_rows(p), :],
            recv_rho.at[pl.ds(pl.multiple_of((ylo * DOMAINS + d) * 16, 16), 16), :],
            fwd_send, rho_recv, device_id=owner_dev(p), device_id_type=MESH,
        )

    def start_all(make, count):
        def one(j, carry):
            make(j).start()
            return carry

        lax.fori_loop(0, count, one, 0)

    start_all(send_ion, 25)

    rho_total = taylor(4)
    psi_copy = pltpu.make_async_copy(raw.at[pl.ds(0, 2800), :], psi_out, out_sem.at[0])
    psi_copy.start()

    forward_z(rho_cols)
    forward_y(e_rho, range(7))
    put_total(e_rho, rho_total)
    start_all(send_rho, PAIRS)

    def share_sum(part):
        return pltpu.make_async_remote_copy(
            rho_chip.at[pl.ds(core * 20 + 15 * part, 15 - 10 * part)],
            rho_y.at[pl.ds(15 * part, 15 - 10 * part)],
            y_send.at[part], y_recv.at[part], device_id=across, device_id_type=MESH,
        )

    share_sum(0).start()

    def await_bytes(ref, sem):
        pltpu.make_async_copy(ref, ref, sem).wait()

    def send_back(j):
        q = (j + chip) & (CHIPS - 1)
        return pltpu.make_async_remote_copy(
            result.at[pl.ds(pl.multiple_of((q >> 1) * 16, 16), 16), :],
            spec.at[pl.ds(pl.multiple_of((2 * pair_of + core) * 16, 16), 16), :],
            back_send, back_recv,
            device_id=dev((q & 1) * 2 + other, q >> 1), device_id_type=MESH,
        )

    @pl.when(is_owner)
    def _():
        await_bytes(recv_ion, ion_recv)
        await_bytes(recv_rho, rho_recv)
        ions = recv_ion[...].reshape(DOMAINS, 2, 8, 128)
        dens = recv_rho[...].reshape(2, DOMAINS, 2, 8, 128)
        dens = dens[0] + dens[1]
        sub8 = lax.broadcasted_iota(i32, (8, 128), 0)

        def total_of(array):
            rows = jnp.sum(array[:, 0], axis=0)
            return jnp.sum(jnp.where(sub8 == 7, rows, 0.0), axis=(0, 1), keepdims=True)

        scale = total_of(dens) / total_of(ions)
        charge = dens - scale.reshape(1, 1, 1, 1) * ions
        right = jnp.concatenate(
            [charge[:, 0].reshape(256, 128), charge[:, 1].reshape(256, 128)], axis=1
        )
        waves = dot(x_fwd[...], stack_right(right)) * coulomb[...]
        w_high, w_low = split(waves)
        back = dot(x_inv[0], w_high) + (dot(x_inv[0], w_low) + dot(x_inv[1], w_high))
        result[...] = jnp.stack(
            [back[:, 0:128].reshape(DOMAINS, 8, 128), back[:, 128:256].reshape(DOMAINS, 8, 128)],
            axis=1,
        ).reshape(DOMAINS * 16, 128)
        start_all(send_back, CHIPS)

    share_sum(1).start()

    def root(i, carry):
        value = (3.0 / math.pi) * (rho_chip[core * 20 + i] + rho_y[i])
        positive = value > 1.0e-37
        safe = jnp.where(positive, value, 1.0)
        guess = jnp.exp(jnp.log(safe) * (1.0 / 3.0))
        guess = (2.0 * guess + safe / (guess * guess)) * (1.0 / 3.0)
        xc[core * 20 + i] = jnp.where(positive, guess, 0.0)
        return carry

    def share_root(part):
        rows = pl.ds(core * 20 + 15 * part, 15 - 10 * part)
        return pltpu.make_async_remote_copy(
            xc.at[rows], xc.at[rows], xc_send.at[part], xc_recv.at[part],
            device_id=partner, device_id_type=MESH,
        )

    share_sum(0).wait_recv()
    lax.fori_loop(0, 15, root, 0)
    share_root(0).start()

    await_bytes(spec.at[pl.ds(0, 800), :], back_recv)

    halves_of = spec.reshape(PAIRS, 32, 128).at[:, pl.ds(pl.multiple_of(other * 16, 16), 16), :]
    swap = pltpu.make_async_remote_copy(
        halves_of, halves_of, mid_send, mid_recv, device_id=partner, device_id_type=MESH
    )
    swap.start()
    share_sum(1).wait_recv()
    lax.fori_loop(15, 20, root, 0)
    share_root(1).start()
    await_bytes(spec.at[pl.ds(0, 800), :], mid_recv)

    for slot in range(7):
        rows = pl.ds(slot, SIDE, stride=8)
        main = spec[rows, :]
        tail = spec[pl.ds(SIDE * 8 + slot, 40, stride=8), :]
        parts = [tail] + [pltpu.roll(tail, 128 - 32 * j, 1) for j in range(1, 4)]
        right = jnp.concatenate([main, jnp.concatenate(parts, axis=0)], axis=1)
        out = dot(iy[...], stack_right(right))
        za[rows, :] = out[:, 0:128]
        zb[rows, :] = out[:, 128:256]
    carried = None
    for r in range(4):
        left = jnp.concatenate(
            [za[r * 320 : (r + 1) * 320, :], zb[r * 320 : (r + 1) * 320, :]], axis=1
        )
        high, low = split(left)
        out = dot_t(high, fz[r, 0:256, :] ) + dot_t(high, fz[r, 256:512, :])
        out = out + dot_t(low, fz[r, 0:256, :])
        piece = out[:, 0:128]
        if carried is not None:
            piece = piece + carried
        hsc[r] = piece
        carried = out[:, 128:256]
    hsc[4] = carried

    share_root(0).wait_recv()
    share_root(1).wait_recv()

    def finish(g, carry):
        for j in range(5):
            value = hsc[j, rows_of(g), :] - xc[g, :, 128 * j : 128 * j + 128]
            value = jnp.where(half[j, rows_of(g), :] > 0.0, value, 0.0)
            field[:, lanes_of(g, j)] = value[0:7, :]
        return carry

    field_copies = []
    for part in range(4):
        lax.fori_loop(10 * part, 10 * part + 10, finish, 0)
        lanes = pl.ds(6400 * part, 6400)
        field_copies.append(
            pltpu.make_async_copy(field.at[:, lanes], field_out.at[:, lanes], out_sem.at[1 + part])
        )
        field_copies[-1].start()

    for k in range(TERMS):
        def drain(ch, carry, k=k):
            to_low, to_high = edge_sends(k, ch)

            @pl.when(has_low)
            def _():
                to_low.wait_send()

            @pl.when(has_high)
            def _():
                to_high.wait_send()

            return carry

        lax.fori_loop(0, CHUNKS, drain, 0)

    def drain_rho(ch, carry):
        share_rho(ch).wait_send()
        return carry

    lax.fori_loop(0, CHUNKS, drain_rho, 0)
    for part in range(2):
        share_sum(part).wait_send()
        share_root(part).wait_send()
    await_bytes(e_ion.at[pl.ds(0, 400), :], ion_send)
    await_bytes(e_rho.at[pl.ds(0, 800), :], fwd_send)
    await_bytes(spec.at[pl.ds(0, 800), :], mid_send)

    @pl.when(is_owner)
    def _():
        await_bytes(recv_rho, back_send)

    psi_copy.wait()
    for copy in field_copies:
        copy.wait()


def hand_over(psi_in, field_in, psi_out, field_out, psi_buf, field_buf, sems):
    moves = []
    for i in range(4):
        rows = pl.ds(704 * i, 704 if i < 3 else 688)
        moves.append((psi_in.at[rows, :], psi_buf.at[rows, :], psi_out.at[rows, :]))
    for i in range(2):
        lanes = pl.ds(12800 * i, 12800)
        moves.append((field_in.at[:, lanes], field_buf.at[:, lanes], field_out.at[:, lanes]))
    reads = [pltpu.make_async_copy(a, b, sems.at[0, i]) for i, (a, b, _) in enumerate(moves)]
    writes = [pltpu.make_async_copy(b, c, sems.at[1, i]) for i, (_, b, c) in enumerate(moves)]
    for read in reads:
        read.start()
    for read, write in zip(reads, writes):
        read.wait()
        write.start()
    for write in writes:
        write.wait()


def step(orbitals, occupation, potential, background, layer_start):
    tabs = [jnp.asarray(t) for t in tables()]
    vmem = lambda *shape: pltpu.VMEM(shape, f32)
    dma = pltpu.SemaphoreType.DMA
    anyspace = pl.BlockSpec(memory_space=pl.ANY)
    smem = pl.BlockSpec(memory_space=pltpu.SMEM)
    edge = (TERMS, CHUNKS, 2, 5, CHUNK_GROUPS, 128)
    cube = (GROUPS, 8, LANES)
    columns = (1600, 128)
    tile5 = (5, 8 * GROUPS, 128)
    padded = (2, 5, 8 * GROUPS + 16, 128)
    scratch = [
        vmem(3000, 128), vmem(LAYERS, PLANE), vmem(LAYERS, PLANE),
        *[pltpu.VMEM(t.shape, bf16) for t in tabs],
        pltpu.VMEM((4, 768, 256), bf16),
        vmem(*padded), vmem(*padded), vmem(2, *tile5), vmem(*tile5), vmem(*tile5), vmem(*tile5),
        vmem(*edge), vmem(*edge), vmem(*edge), vmem(*edge),
        vmem(*cube), vmem(*cube), vmem(*cube), vmem(*tile5), vmem(20, 8, LANES), vmem(*cube),
        vmem(1280, 128), vmem(1280, 128), vmem(960, 128), vmem(960, 128),
        vmem(1024, 128), vmem(512, 128), vmem(512, 128), vmem(*columns),
        vmem(*tile5), vmem(LAYERS, PLANE),
        pltpu.VMEM((SIDE, 768), bf16), pltpu.VMEM((2, 256, SIDE), bf16), vmem(SIDE, 256),
        dma((3,)), dma((5,)), dma((5,)),
        dma((TERMS, CHUNKS)), dma((TERMS, CHUNKS)), dma((TERMS, CHUNKS)), dma((TERMS, CHUNKS)),
        dma((CHUNKS,)), dma((CHUNKS,)),
        *[dma((2,)) for _ in range(4)],
        *[dma(()) for _ in range(8)],
        pltpu.SemaphoreType.REGULAR, pltpu.SemaphoreType.REGULAR,
    ]
    psi, field = pl.pallas_call(
        kernel,
        out_shape=(
            jax.ShapeDtypeStruct((2800, 128), f32),
            jax.ShapeDtypeStruct((LAYERS, PLANE), f32),
        ),
        in_specs=[smem, smem] + [anyspace] * 8,
        out_specs=(anyspace, anyspace),
        scratch_shapes=scratch,
        compiler_params=pltpu.CompilerParams(
            collective_id=0, has_side_effects=True, vmem_limit_bytes=60 * 1024 * 1024
        ),
    )(
        layer_start, occupation, orbitals.reshape(2800, 128), potential, background, *tabs
    )
    psi, field = pl.pallas_call(
        hand_over,
        out_shape=(
            jax.ShapeDtypeStruct((2800, 128), f32),
            jax.ShapeDtypeStruct((LAYERS, PLANE), f32),
        ),
        in_specs=[anyspace, anyspace],
        out_specs=(anyspace, anyspace),
        scratch_shapes=[vmem(2800, 128), vmem(LAYERS, PLANE), dma((2, 6))],
        compiler_params=pltpu.CompilerParams(vmem_limit_bytes=60 * 1024 * 1024),
    )(psi, field)
    return psi.reshape(2, 1, LAYERS, PLANE), field


def solution(mesh):
    return jax.shard_map(
        step,
        mesh=mesh,
        in_specs=(
            P(None, "state", "domain", None),
            P("state"),
            P("domain", None),
            P("domain", None),
            P(),
        ),
        out_specs=(P(None, "state", "domain", None), P("domain", None)),
        check_vma=False,
    )
```

```python
import functools
import math

import jax
import jax.numpy as jnp
import numpy as np
from jax import lax
from jax.experimental import pallas as pl
from jax.experimental.pallas import tpu as pltpu
from jax.sharding import PartitionSpec as P

SIDE = 160
SLAB = 5
TERMS = 4
LAYERS = 7
PLANE = SIDE * SIDE
GROUPS = 40
LANES = 640
CHUNKS = 5
CHUNK_GROUPS = 8
OWNERS = 100
PAIRS = 50
DOMAINS = 32
STATES = 4
CHIPS = 64

time_step = 0.3
four_pi = 4.0 * math.pi
two_pi = 2.0 * math.pi
MESH = pl.DeviceIdType.MESH
f32 = jnp.float32
i32 = jnp.int32
bf16 = jnp.bfloat16


def halves(table):
    table = np.asarray(table, np.float32)
    high = table.astype(bf16)
    low = (table - high.astype(np.float32)).astype(bf16)
    return np.stack([high, low])


def real_basis():
    n = SIDE
    j = np.arange(n)
    rows = []
    for i in range(n):
        if i == 0:
            rows.append(np.full(n, math.sqrt(1.0 / n)))
        elif i < n // 2:
            rows.append(math.sqrt(2.0 / n) * np.cos(2 * np.pi * ((i * j) % n) / n))
        elif i == n // 2:
            rows.append(math.sqrt(1.0 / n) * np.where(j % 2 == 0, 1.0, -1.0))
        else:
            m = i - n // 2
            rows.append(math.sqrt(2.0 / n) * np.sin(2 * np.pi * ((m * j) % n) / n))
    return np.stack(rows)


def tables():
    q = real_basis()
    side_table = np.zeros((SIDE, 256))
    side_table[:, :SIDE] = q.T
    order = np.array([4 * g + r for r in range(4) for g in range(GROUPS)])
    forward_y = q[:, order]
    x_table = np.zeros((SIDE, 256))
    x_table[:, :SIDE] = q
    x_back = np.zeros((256, SIDE))
    x_back[:SIDE, :] = q.T
    half_y = np.zeros((2, 96, SIDE))
    for which in range(2):
        for j in range(4):
            for q in range(20):
                half_y[which, 24 * j + q] = forward_y[40 * j + 4 * (q // 2) + 2 * which + q % 2]
    high, low = halves(half_y)
    left_y = np.concatenate([high, high, low], axis=2)
    high, low = halves(forward_y.T)
    left_back = np.concatenate([high, high, low], axis=1)
    return [halves(side_table), left_y, left_back, halves(x_table), halves(x_back)]


def split(value):
    high = value.astype(bf16)
    low = (value - high.astype(f32)).astype(bf16)
    return high, low


def dot(a, b):
    return jnp.dot(a, b, preferred_element_type=f32)


def dot_t(a, b):
    dims = (((1,), (1,)), ((), ()))
    return lax.dot_general(a, b, dims, preferred_element_type=f32)


def stack_left(value, axis=1):
    high, low = split(value)
    return jnp.concatenate([high, high, low], axis=axis)


def stack_right(value, axis=0):
    high, low = split(value)
    return jnp.concatenate([high, low, high], axis=axis)


def kernel(
    starts, occ, orb_hbm, pot_hbm, bg_hbm, qz_hbm, fy_hbm, iy_hbm, xt_hbm, xb_hbm,
    psi_out, field_out,
    raw, pot, bg, qz, fy, iy, xt, xb, fz,
    cur_a, cur_b, psi, diag, half, ion,
    send_lo, send_hi, halo_lo, halo_hi,
    rho_own, rho_rx, rho_chip, rho_cols, rho_y, xc,
    za, zb, e_rho, e_ion, recv_rho, recv_ion, result, spec, hsc, field,
    x_fwd, x_inv, coulomb,
    load_sem, table_sem, out_sem,
    send_lo_sem, send_hi_sem, recv_lo_sem, recv_hi_sem,
    part_send, part_recv, y_send, y_recv, xc_send, xc_recv,
    fwd_send, rho_recv, ion_send, ion_recv, back_send, back_recv, mid_send, mid_recv,
    ready_a, ready_b,
):
    s = lax.axis_index("state")
    d = lax.axis_index("domain")
    core = s & 1
    ylo = s >> 1
    chip = d * 2 + ylo

    def dev(state, domain):
        return {"state": state, "domain": domain}

    partner = dev(ylo * 2 + 1 - core, d)
    across = dev((1 - ylo) * 2 + core, d)
    has_low = d > 0
    has_high = d < DOMAINS - 1
    low_dev = dev(s, jnp.maximum(d - 1, 0))
    high_dev = dev(s, jnp.minimum(d + 1, DOMAINS - 1))
    octet = d >> 3
    place = d & 7

    barrier = pltpu.get_barrier_semaphore()

    def greet(state, domain):
        pl.semaphore_signal(barrier, inc=1, device_id=dev(state, domain), device_id_type=MESH)

    for step in range(1, 8):
        greet(s, octet * 8 + ((place + step) & 7))
    for step in range(1, 4):
        greet((s + step) & 3, d)
        greet(s, (d + 8 * step) & (DOMAINS - 1))
    cross_low = jnp.logical_and(place == 0, has_low)
    cross_high = jnp.logical_and(place == 7, has_high)

    @pl.when(cross_low)
    def _():
        greet(s, jnp.maximum(d - 1, 0))

    @pl.when(cross_high)
    def _():
        greet(s, jnp.minimum(d + 1, DOMAINS - 1))

    orb_copy = pltpu.make_async_copy(orb_hbm, raw.at[pl.ds(0, 2800), :], load_sem.at[0])
    pot_copy = pltpu.make_async_copy(pot_hbm, pot, load_sem.at[1])
    bg_copy = pltpu.make_async_copy(bg_hbm, bg, load_sem.at[2])
    table_copies = [
        pltpu.make_async_copy(src, dst, table_sem.at[i])
        for i, (src, dst) in enumerate(
            ((qz_hbm, qz), (fy_hbm, fy), (iy_hbm, iy), (xt_hbm, xt), (xb_hbm, xb))
        )
    ]
    for copy in [orb_copy, pot_copy, bg_copy] + table_copies:
        copy.start()

    own_start = starts[d]
    thickness = starts[d + 1] - own_start
    top_row = jnp.clip(thickness - 1, 0, LAYERS - 1)
    lane = lax.broadcasted_iota(i32, (8, 128), 1)
    sub = lax.broadcasted_iota(i32, (8, 128), 0)
    radius = float((SIDE - 2) ** 2)
    x_off = (2 * (own_start + sub) - (SIDE - 1)).astype(f32)
    x_square = jnp.where(sub < thickness, x_off * x_off, 1.0e9)
    yz_parts = []
    for j in range(5):
        flat = lane + 128 * j
        y_low = (
            (flat >= SIDE).astype(i32)
            + (flat >= 2 * SIDE).astype(i32)
            + (flat >= 3 * SIDE).astype(i32)
        )
        z_off = (2 * (flat - SIDE * y_low) - (SIDE - 1)).astype(f32)
        yz_parts.append(((2 * y_low - (SIDE - 1)).astype(f32), x_square + z_off * z_off))
    is_spare = sub == 7
    is_above = sub == top_row + 1
    first_lane = lane == 0
    last_lane = lane == 127
    low_lanes = lane < 32
    high_lanes = lane >= 96

    def inside(g, j):
        y_base, xz_square = yz_parts[j]
        y_off = y_base + (8 * g).astype(f32)
        return y_off * y_off + xz_square <= radius

    def lanes_of(g, j):
        return pl.ds(pl.multiple_of(g * LANES + 128 * j, 128), 128)

    def rows_of(g):
        return pl.ds(pl.multiple_of(g * 8, 8), 8)

    def rows7_of(g):
        return pl.ds(pl.multiple_of(g * 8, 8), 7)

    def edge_sends(k, ch):
        to_low = pltpu.make_async_remote_copy(
            send_lo.at[k, ch], halo_hi.at[k, ch], send_lo_sem.at[k, ch], recv_hi_sem.at[k, ch],
            device_id=low_dev, device_id_type=MESH,
        )
        to_high = pltpu.make_async_remote_copy(
            send_hi.at[k, ch], halo_lo.at[k, ch], send_hi_sem.at[k, ch], recv_lo_sem.at[k, ch],
            device_id=high_dev, device_id_type=MESH,
        )
        return to_low, to_high

    def start_edges(k, ch):
        to_low, to_high = edge_sends(k, ch)

        @pl.when(has_low)
        def _():
            to_low.start()

        @pl.when(has_high)
        def _():
            to_high.start()

    def await_edges(k, ch):
        to_low, to_high = edge_sends(k, ch)

        @pl.when(has_low)
        def _():
            to_high.wait_recv()

        @pl.when(has_high)
        def _():
            to_low.wait_recv()

    zero = jnp.zeros((8, 128), f32)
    for cur in (cur_a, cur_b):
        for c in range(2):
            for j in range(5):
                cur[c, j, 0:8, :] = zero
                cur[c, j, 8 * GROUPS + 8 : 8 * GROUPS + 16, :] = zero

    def pick_edges(cur, k, ch):
        base = (ch * CHUNK_GROUPS + 1) * 8
        for c in range(2):
            for j in range(5):
                view = cur.at[c, j]
                send_lo[k, ch, c, j] = view[pl.ds(base, CHUNK_GROUPS, stride=8), :]
                send_hi[k, ch, c, j] = view[pl.ds(base + top_row, CHUNK_GROUPS, stride=8), :]

    @pl.when(jnp.logical_not(has_low))
    def _():
        halo_lo[...] = jnp.zeros(halo_lo.shape, f32)

    @pl.when(jnp.logical_not(has_high))
    def _():
        halo_hi[...] = jnp.zeros(halo_hi.shape, f32)

    orb_copy.wait()
    pot_copy.wait()

    def first_chunk(ch, carry):
        def first(gi, inner):
            for step_g in range(2):
                g = ch * CHUNK_GROUPS + gi * 2 + step_g
                for j in range(5):
                    keep = inside(g, j)
                    mask = jnp.where(keep, 1.0, 0.0)
                    half[j, rows_of(g), :] = 0.5 * mask
                    diag[j, rows_of(g), :] = zero
                    diag[j, rows7_of(g), :] = (3.0 + pot[:, lanes_of(g, j)]) * mask[0:7, :]
                    for c in range(2):
                        value = raw[pl.ds(c * 1400 + 5 * g + j, 8, stride=200), :]
                        value = jnp.where(keep, value, 0.0)
                        cur_a[c, j, rows_of(g + 1), :] = value
                        psi[c, j, rows_of(g), :] = value
            return inner

        lax.fori_loop(0, CHUNK_GROUPS // 2, first, 0)
        pick_edges(cur_a, 0, ch)
        return carry

    lax.fori_loop(0, CHUNKS, first_chunk, 0)
    pl.semaphore_wait(
        barrier, 13 + jnp.where(cross_low, 1, 0) + jnp.where(cross_high, 1, 0)
    )


    def send_first(ch, carry):
        start_edges(0, ch)
        return carry

    lax.fori_loop(0, CHUNKS, send_first, 0)

    for step in range(1, 4):
        pl.semaphore_signal(ready_a, inc=1, device_id=dev((s + step) & 3, d), device_id_type=MESH)

    span = 4

    def taylor(k):
        factor = time_step / k
        src, dst = (cur_a, cur_b) if k % 2 else (cur_b, cur_a)
        count = 5 * span

        def chunk(ch, carry):
            await_edges(k - 1, ch)

            def block(bi, inner):
                g0 = ch * CHUNK_GROUPS + bi * span

                def tile(c, v):
                    return src[c, v % 5, rows_of(g0 + 1 + v // 5), :]

                def turned(own, amount, cache):
                    def at(v):
                        if v not in cache:
                            cache[v] = pltpu.roll(own(v), amount, 1)
                        return cache[v]

                    return at

                for c in range(2):
                    tiles = {}

                    def own(v, c=c, tiles=tiles):
                        if v not in tiles:
                            tiles[v] = tile(c, v)
                        return tiles[v]

                    right1, left1, right32, left32 = (
                        turned(own, amount, {}) for amount in (1, 127, 32, 96)
                    )
                    to = 1 - c
                    scale = -factor if to else factor
                    for v in range(count):
                        j, gi = v % 5, bi * span + v // 5
                        g = g0 + v // 5
                        rows = rows_of(g)
                        near = jnp.where(first_lane, right1(v - 1), right1(v)) + jnp.where(
                            last_lane, left1(v + 1), left1(v)
                        )
                        far = jnp.where(low_lanes, right32(v - 2), right32(v - 1)) + jnp.where(
                            high_lanes, left32(v + 2), left32(v + 1)
                        )
                        low = jnp.broadcast_to(
                            halo_lo[k - 1, ch, c, j, pl.ds(gi, 1), :], (8, 128)
                        )
                        high = jnp.broadcast_to(
                            halo_hi[k - 1, ch, c, j, pl.ds(gi, 1), :], (8, 128)
                        )
                        stacked = pltpu.roll(
                            jnp.where(is_spare, low, own(v)), 1, 0
                        ) + pltpu.roll(jnp.where(is_above, high, own(v)), 7, 0)
                        fresh = scale * (
                            diag[j, rows, :] * own(v)
                            - half[j, rows, :] * ((near + far) + stacked)
                        )
                        value = psi[to, j, rows, :] + fresh
                        if k < TERMS:
                            dst[to, j, rows_of(g + 1), :] = fresh
                            psi[to, j, rows, :] = value
                        else:
                            raw[pl.ds(to * 1400 + 5 * g + j, 7, stride=200), :] = value[0:7, :]
                            cols = slice(128 * j, 128 * j + 128)
                            square = occ[0] * (value * value)
                            if c:
                                square = rho_own[g, :, cols] + square
                            rho_own[g, :, cols] = square
                return inner

            lax.fori_loop(0, CHUNK_GROUPS // span, block, 0)
            if k < TERMS:
                pick_edges(dst, k, ch)
                start_edges(k, ch)
                return carry
            share_rho(ch).start()
            return chip_sum(ch - 1, ch > 0, carry)

        if k < TERMS:
            return lax.fori_loop(0, CHUNKS, chunk, 0)
        return chip_sum(CHUNKS - 1, None, lax.fori_loop(0, CHUNKS, chunk, zero))

    def chip_sum(ch, live, acc):
        if live is None:
            share_rho(ch).wait_recv()
        else:

            @pl.when(live)
            def _():
                share_rho(ch).wait_recv()

        def group(gi, inner):
            g = ch * CHUNK_GROUPS + gi
            for j in range(5):
                cols = slice(128 * j, 128 * j + 128)
                value = rho_own[g, :, cols] + rho_rx[g, :, cols]
                rho_chip[g, :, cols] = value
                rho_cols[j, rows_of(g), :] = value
                inner = inner + value
            return inner

        count = CHUNK_GROUPS if live is None else jnp.where(live, CHUNK_GROUPS, 0)
        return lax.fori_loop(0, count, group, acc)

    def share_rho(ch):
        rows = pl.ds(ch * CHUNK_GROUPS, CHUNK_GROUPS)
        return pltpu.make_async_remote_copy(
            rho_own.at[rows], rho_rx.at[rows], part_send.at[ch], part_recv.at[ch],
            device_id=partner, device_id_type=MESH,
        )

    def forward_z(src):
        parts = [split(src[j]) for j in range(5)]
        for r in range(4):
            high, low = (
                jnp.concatenate([parts[r][i], parts[r + 1][i]], axis=1) for i in range(2)
            )
            out = dot(jnp.concatenate([high, high, low], axis=1), fz[r])
            za[r * 320 : (r + 1) * 320, :] = out[:, 0:128]
            zb[r * 320 : (r + 1) * 320, :] = out[:, 128:256]

    other = 1 - core

    def forward_y(dst, slots):
        table = fy[other]
        for slot in slots:
            rows = pl.ds(slot, SIDE, stride=8)
            right = jnp.concatenate([za[rows, :], zb[rows, :]], axis=1)
            out = dot(table, stack_right(right))
            dst[pl.ds(slot, 96, stride=8), :] = out[:, 0:128]
            tail = out[:, 128:256]
            packed = tail[0:24, :]
            for j in range(1, 4):
                packed = packed + pltpu.roll(tail[24 * j : 24 * j + 24, :], 32 * j, 1)
            dst[pl.ds(96 * 8 + slot, 24, stride=8), :] = packed

    def put_total(dst, partial):
        total = jnp.broadcast_to(jnp.sum(partial, axis=0, keepdims=True), (120, 128))
        dst[pl.ds(7, 120, stride=8), :] = total

    pair_of = (chip * 25 + 31) >> 5
    is_owner = jnp.logical_and(lax.div(pair_of * 32, 25) == chip, pair_of < PAIRS)

    def build_x_tables():
        @pl.when(is_owner)
        def _():
            lane256 = lax.broadcasted_iota(i32, (SIDE, 256), 1)
            row160 = lax.broadcasted_iota(i32, (SIDE, 256), 0)
            lane_row = lax.broadcasted_iota(i32, (8, 256), 1)
            slot_row = lane_row % 8
            dom_row = lane_row // 8
            where_x = jnp.full((8, 256), -1, i32)
            pieces = []
            sub256 = lax.broadcasted_iota(i32, (8, 256), 0)
            for k in range(DOMAINS):
                first_x = starts[k]
                count = starts[k + 1] - first_x
                where_x = jnp.where(
                    jnp.logical_and(dom_row == k, slot_row < count), first_x + slot_row, where_x
                )
                hit = jnp.logical_and(lane_row == first_x + sub256, sub256 < count)
                pieces.append(jnp.where(hit, 1.0, 0.0))
            select_back = jnp.concatenate(pieces, axis=0).astype(bf16)
            wide_x = jnp.broadcast_to(where_x[0:1, :], (256, 256))
            row256 = lax.broadcasted_iota(i32, (256, 256), 0)
            select = jnp.where(wide_x == row256, 1.0, 0.0).astype(bf16)
            x_high, x_low = (dot(xt[i], select).astype(bf16) for i in range(2))
            x_fwd[...] = jnp.concatenate([x_high, x_high, x_low], axis=1)
            for i in range(2):
                x_inv[i] = dot(select_back, xb[i]).astype(bf16)
            o = 2 * pair_of + core
            unit = 2 * o + lane256 // 128
            low_lane = lane256 % 128
            is_tail = unit >= SIDE
            ky = jnp.where(is_tail, 40 * (low_lane // 32) + unit - SIDE, unit)
            kz = jnp.where(is_tail, 128 + low_lane % 32, low_lane)

            def wave(index):
                folded = jnp.where(2 * index <= SIDE, index, index - SIDE // 2)
                number = folded.astype(f32) * (two_pi / SIDE)
                return number * number

            squared = wave(row160) + wave(ky) + wave(kz)
            coulomb[...] = jnp.where(squared > 0, four_pi / jnp.where(squared > 0, squared, 1.0), 0.0)


    bg_copy.wait()

    def ion_group(g, acc):
        for j in range(5):
            weight = 2.0 * half[j, rows_of(g), :]
            ion[j, rows_of(g), :] = zero
            ion[j, rows7_of(g), :] = bg[:, lanes_of(g, j)] * weight[0:7, :]
            acc = acc + ion[j, rows_of(g), :]
        return acc

    ion_total = lax.fori_loop(0, GROUPS, ion_group, zero)
    for copy in table_copies:
        copy.wait()
    fz[...] = jnp.zeros(fz.shape, bf16)
    for i, which in enumerate((0, 1, 0)):
        for r in range(4):
            fz[r, 256 * i + 32 * r : 256 * i + 32 * r + SIDE, :] = qz[which]
    forward_z(ion)

    forward_y(e_ion, range(0, 4))
    taylor(1)
    forward_y(e_ion, range(4, 7))
    put_total(e_ion, ion_total)

    pl.semaphore_wait(ready_a, 3)
    for step in range(1, 4):
        pl.semaphore_signal(
            ready_b, inc=1, device_id=dev(s, (d + 8 * step) & (DOMAINS - 1)), device_id_type=MESH
        )

    taylor(2)
    build_x_tables()
    taylor(3)
    pl.semaphore_wait(ready_b, 3)

    def owner_dev(p):
        place_of = p + ((p * (7 * 5243)) >> 17)
        return dev((place_of & 1) * 2 + other, place_of >> 1)

    def sent_rows(p):
        tens = (p * 205) >> 11
        return pl.ds(pl.multiple_of((4 * tens + 2 * p) * 8, 16), 16)

    def column_rows(p, half_of):
        return pl.ds(pl.multiple_of((2 * p + half_of) * 16, 16), 16)

    def wrap(value, count):
        return jnp.where(value >= count, value - count, value)

    ion_first = lax.rem(d, jnp.int32(25))
    rho_first = (chip * 25) >> 5

    def send_ion(j):
        p = 2 * wrap(j + ion_first, 25) + ylo
        return pltpu.make_async_remote_copy(
            e_ion.at[sent_rows(p), :],
            recv_ion.at[pl.ds(pl.multiple_of(d * 16, 16), 16), :],
            ion_send, ion_recv, device_id=owner_dev(p), device_id_type=MESH,
        )

    def send_rho(j):
        p = wrap(j + rho_first, PAIRS)
        return pltpu.make_async_remote_copy(
            e_rho.at[sent_rows(p), :],
            recv_rho.at[pl.ds(pl.multiple_of((ylo * DOMAINS + d) * 16, 16), 16), :],
            fwd_send, rho_recv, device_id=owner_dev(p), device_id_type=MESH,
        )

    def start_all(make, count):
        def one(j, carry):
            make(j).start()
            return carry

        lax.fori_loop(0, count, one, 0)

    start_all(send_ion, 25)

    rho_total = taylor(4)
    psi_copy = pltpu.make_async_copy(raw.at[pl.ds(0, 2800), :], psi_out, out_sem.at[0])
    psi_copy.start()

    forward_z(rho_cols)
    forward_y(e_rho, range(7))
    put_total(e_rho, rho_total)
    start_all(send_rho, PAIRS)

    def share_sum(part):
        return pltpu.make_async_remote_copy(
            rho_chip.at[pl.ds(core * 20 + 15 * part, 15 - 10 * part)],
            rho_y.at[pl.ds(15 * part, 15 - 10 * part)],
            y_send.at[part], y_recv.at[part], device_id=across, device_id_type=MESH,
        )

    share_sum(0).start()

    def await_bytes(ref, sem):
        pltpu.make_async_copy(ref, ref, sem).wait()

    def send_back(j):
        q = (j + chip) & (CHIPS - 1)
        return pltpu.make_async_remote_copy(
            result.at[pl.ds(pl.multiple_of((q >> 1) * 16, 16), 16), :],
            spec.at[pl.ds(pl.multiple_of((2 * pair_of + core) * 16, 16), 16), :],
            back_send, back_recv,
            device_id=dev((q & 1) * 2 + other, q >> 1), device_id_type=MESH,
        )

    @pl.when(is_owner)
    def _():
        await_bytes(recv_ion, ion_recv)
        await_bytes(recv_rho, rho_recv)
        ions = recv_ion[...].reshape(DOMAINS, 2, 8, 128)
        dens = recv_rho[...].reshape(2, DOMAINS, 2, 8, 128)
        dens = dens[0] + dens[1]
        sub8 = lax.broadcasted_iota(i32, (8, 128), 0)

        def total_of(array):
            rows = jnp.sum(array[:, 0], axis=0)
            return jnp.sum(jnp.where(sub8 == 7, rows, 0.0), axis=(0, 1), keepdims=True)

        scale = total_of(dens) / total_of(ions)
        charge = dens - scale.reshape(1, 1, 1, 1) * ions
        right = jnp.concatenate(
            [charge[:, 0].reshape(256, 128), charge[:, 1].reshape(256, 128)], axis=1
        )
        waves = dot(x_fwd[...], stack_right(right)) * coulomb[...]
        w_high, w_low = split(waves)
        back = dot(x_inv[0], w_high) + (dot(x_inv[0], w_low) + dot(x_inv[1], w_high))
        result[...] = jnp.stack(
            [back[:, 0:128].reshape(DOMAINS, 8, 128), back[:, 128:256].reshape(DOMAINS, 8, 128)],
            axis=1,
        ).reshape(DOMAINS * 16, 128)
        start_all(send_back, CHIPS)

    share_sum(1).start()

    def root(i, carry):
        value = (3.0 / math.pi) * (rho_chip[core * 20 + i] + rho_y[i])
        positive = value > 1.0e-37
        safe = jnp.where(positive, value, 1.0)
        guess = jnp.exp(jnp.log(safe) * (1.0 / 3.0))
        guess = (2.0 * guess + safe / (guess * guess)) * (1.0 / 3.0)
        xc[core * 20 + i] = jnp.where(positive, guess, 0.0)
        return carry

    def share_root(part):
        rows = pl.ds(core * 20 + 15 * part, 15 - 10 * part)
        return pltpu.make_async_remote_copy(
            xc.at[rows], xc.at[rows], xc_send.at[part], xc_recv.at[part],
            device_id=partner, device_id_type=MESH,
        )

    share_sum(0).wait_recv()
    lax.fori_loop(0, 15, root, 0)
    share_root(0).start()

    await_bytes(spec.at[pl.ds(0, 800), :], back_recv)

    halves_of = spec.reshape(PAIRS, 32, 128).at[:, pl.ds(pl.multiple_of(other * 16, 16), 16), :]
    swap = pltpu.make_async_remote_copy(
        halves_of, halves_of, mid_send, mid_recv, device_id=partner, device_id_type=MESH
    )
    swap.start()
    share_sum(1).wait_recv()
    lax.fori_loop(15, 20, root, 0)
    share_root(1).start()
    await_bytes(spec.at[pl.ds(0, 800), :], mid_recv)

    for slot in range(7):
        rows = pl.ds(slot, SIDE, stride=8)
        main = spec[rows, :]
        tail = spec[pl.ds(SIDE * 8 + slot, 40, stride=8), :]
        parts = [tail] + [pltpu.roll(tail, 128 - 32 * j, 1) for j in range(1, 4)]
        right = jnp.concatenate([main, jnp.concatenate(parts, axis=0)], axis=1)
        out = dot(iy[...], stack_right(right))
        za[rows, :] = out[:, 0:128]
        zb[rows, :] = out[:, 128:256]
    carried = None
    for r in range(4):
        left = jnp.concatenate(
            [za[r * 320 : (r + 1) * 320, :], zb[r * 320 : (r + 1) * 320, :]], axis=1
        )
        high, low = split(left)
        out = dot_t(high, fz[r, 0:256, :] ) + dot_t(high, fz[r, 256:512, :])
        out = out + dot_t(low, fz[r, 0:256, :])
        piece = out[:, 0:128]
        if carried is not None:
            piece = piece + carried
        hsc[r] = piece
        carried = out[:, 128:256]
    hsc[4] = carried

    share_root(0).wait_recv()
    share_root(1).wait_recv()

    def finish(g, carry):
        for j in range(5):
            value = hsc[j, rows_of(g), :] - xc[g, :, 128 * j : 128 * j + 128]
            value = jnp.where(half[j, rows_of(g), :] > 0.0, value, 0.0)
            field[:, lanes_of(g, j)] = value[0:7, :]
        return carry

    field_copies = []
    for part in range(4):
        lax.fori_loop(10 * part, 10 * part + 10, finish, 0)
        lanes = pl.ds(6400 * part, 6400)
        field_copies.append(
            pltpu.make_async_copy(field.at[:, lanes], field_out.at[:, lanes], out_sem.at[1 + part])
        )
        field_copies[-1].start()

    for k in range(TERMS):
        def drain(ch, carry, k=k):
            to_low, to_high = edge_sends(k, ch)

            @pl.when(has_low)
            def _():
                to_low.wait_send()

            @pl.when(has_high)
            def _():
                to_high.wait_send()

            return carry

        lax.fori_loop(0, CHUNKS, drain, 0)

    def drain_rho(ch, carry):
        share_rho(ch).wait_send()
        return carry

    lax.fori_loop(0, CHUNKS, drain_rho, 0)
    for part in range(2):
        share_sum(part).wait_send()
        share_root(part).wait_send()
    await_bytes(e_ion.at[pl.ds(0, 400), :], ion_send)
    await_bytes(e_rho.at[pl.ds(0, 800), :], fwd_send)
    await_bytes(spec.at[pl.ds(0, 800), :], mid_send)

    @pl.when(is_owner)
    def _():
        await_bytes(recv_rho, back_send)

    psi_copy.wait()
    for copy in field_copies:
        copy.wait()


def hand_over(psi_in, field_in, psi_out, field_out, psi_buf, field_buf, sems):
    moves = []
    for i in range(4):
        rows = pl.ds(704 * i, 704 if i < 3 else 688)
        moves.append((psi_in.at[rows, :], psi_buf.at[rows, :], psi_out.at[rows, :]))
    for i in range(2):
        lanes = pl.ds(12800 * i, 12800)
        moves.append((field_in.at[:, lanes], field_buf.at[:, lanes], field_out.at[:, lanes]))
    reads = [pltpu.make_async_copy(a, b, sems.at[0, i]) for i, (a, b, _) in enumerate(moves)]
    writes = [pltpu.make_async_copy(b, c, sems.at[1, i]) for i, (_, b, c) in enumerate(moves)]
    for read in reads:
        read.start()
    for read, write in zip(reads, writes):
        read.wait()
        write.start()
    for write in writes:
        write.wait()


def step(orbitals, occupation, potential, background, layer_start):
    tabs = [jnp.asarray(t) for t in tables()]
    vmem = lambda *shape: pltpu.VMEM(shape, f32)
    dma = pltpu.SemaphoreType.DMA
    anyspace = pl.BlockSpec(memory_space=pl.ANY)
    smem = pl.BlockSpec(memory_space=pltpu.SMEM)
    edge = (TERMS, CHUNKS, 2, 5, CHUNK_GROUPS, 128)
    cube = (GROUPS, 8, LANES)
    columns = (1600, 128)
    tile5 = (5, 8 * GROUPS, 128)
    padded = (2, 5, 8 * GROUPS + 16, 128)
    scratch = [
        vmem(3000, 128), vmem(LAYERS, PLANE), vmem(LAYERS, PLANE),
        *[pltpu.VMEM(t.shape, bf16) for t in tabs],
        pltpu.VMEM((4, 768, 256), bf16),
        vmem(*padded), vmem(*padded), vmem(2, *tile5), vmem(*tile5), vmem(*tile5), vmem(*tile5),
        vmem(*edge), vmem(*edge), vmem(*edge), vmem(*edge),
        vmem(*cube), vmem(*cube), vmem(*cube), vmem(*tile5), vmem(20, 8, LANES), vmem(*cube),
        vmem(1280, 128), vmem(1280, 128), vmem(960, 128), vmem(960, 128),
        vmem(1024, 128), vmem(512, 128), vmem(512, 128), vmem(*columns),
        vmem(*tile5), vmem(LAYERS, PLANE),
        pltpu.VMEM((SIDE, 768), bf16), pltpu.VMEM((2, 256, SIDE), bf16), vmem(SIDE, 256),
        dma((3,)), dma((5,)), dma((5,)),
        dma((TERMS, CHUNKS)), dma((TERMS, CHUNKS)), dma((TERMS, CHUNKS)), dma((TERMS, CHUNKS)),
        dma((CHUNKS,)), dma((CHUNKS,)),
        *[dma((2,)) for _ in range(4)],
        *[dma(()) for _ in range(8)],
        pltpu.SemaphoreType.REGULAR, pltpu.SemaphoreType.REGULAR,
    ]
    psi, field = pl.pallas_call(
        kernel,
        out_shape=(
            jax.ShapeDtypeStruct((2800, 128), f32),
            jax.ShapeDtypeStruct((LAYERS, PLANE), f32),
        ),
        in_specs=[smem, smem] + [anyspace] * 8,
        out_specs=(anyspace, anyspace),
        scratch_shapes=scratch,
        compiler_params=pltpu.CompilerParams(
            collective_id=0, has_side_effects=True, vmem_limit_bytes=60 * 1024 * 1024
        ),
    )(
        layer_start, occupation, orbitals.reshape(2800, 128), potential, background, *tabs
    )
    psi, field = pl.pallas_call(
        hand_over,
        out_shape=(
            jax.ShapeDtypeStruct((2800, 128), f32),
            jax.ShapeDtypeStruct((LAYERS, PLANE), f32),
        ),
        in_specs=[anyspace, anyspace],
        out_specs=(anyspace, anyspace),
        scratch_shapes=[vmem(2800, 128), vmem(LAYERS, PLANE), dma((2, 6))],
        compiler_params=pltpu.CompilerParams(vmem_limit_bytes=60 * 1024 * 1024),
    )(psi, field)
    return psi.reshape(2, 1, LAYERS, PLANE), field


def solution(mesh):
    return jax.shard_map(
        step,
        mesh=mesh,
        in_specs=(
            P(None, "state", "domain", None),
            P("state"),
            P("domain", None),
            P("domain", None),
            P(),
        ),
        out_specs=(P(None, "state", "domain", None), P("domain", None)),
        check_vma=False,
    )
```
